128 devices in a mesh: dp: 4 (over y), ctx: 32 (over z, x, core).
Axes of the slice: x: 4, y: 4, z: 4, core: 2. Of those that a mesh axis runs over, the one named last changes fastest.
Arguments:
- projected: bfloat16 [4, 4096, 3, 8192], P('dp', 'ctx'), may hold values from -6 to 6
- short_filter: float32 [3, 7, 8192], replicated, may hold values from -2.4 to 2.4
- residues: float32 [512, 16], replicated, may hold values from -0.06 to 0.06
- decay_rates: float32 [512, 16], replicated, may hold values from 2.4414063e-05 to 0.03125
- skip_gain: float32 [8192], replicated, may hold values from 0.5 to 1.5
- cotangent: bfloat16 [4, 4096, 8192], P('dp', 'ctx'), may hold values from -6 to 6
Outputs:
- output: bfloat16 [4, 4096, 8192], P('dp', 'ctx')
- grad_projected: bfloat16 [4, 4096, 3, 8192], P('dp', 'ctx')
- grad_short: float32 [3, 7, 8192], replicated
- grad_skip: float32 [8192], replicated
The draws below stay inside these ranges and needn't reach their ends.
All inputs are finite; a program needn't handle non-finite values.
Results may differ from the reference program's by a relative error of at most 0.001.
Values may be sent and summed in bfloat16 or wider, within the bound.
A program may use at most 320 MiB of HBM per device.

```python
import math
import jax
import jax.numpy as jnp
from jax import lax

D = 8192
POLES = 16
GROUPS = 512
SHORT = 7
BLK = 64
SEQ = 4096
SEQS = 4


def block_levels(key, shape, shards, smallest, top_value):
    loudness, own = 1.0, jax.random.fold_in(key, 6)
    for dim, parts in shards:
        draws = jnp.exp(jax.random.uniform(jax.random.fold_in(own, dim), (parts,), jnp.float32, smallest / len(shards), top_value / len(shards)))
        loudness = loudness * jnp.repeat(draws, shape[dim] // parts).reshape([-1 if axis == dim else 1 for axis in range(len(shape))])
    return loudness


def gaussian(stream_key, extent, scale, bound, shards=(), kind=jnp.bfloat16):
    factor_of = block_levels(stream_key, extent, shards, -0.22, 0.18) if shards else 1.0
    result = jax.random.normal(stream_key, extent, jnp.float32) * scale * factor_of
    return jnp.minimum(jnp.maximum(result, -bound), bound).astype(kind)


def setup_inputs(seed: int = 0) -> dict:
    key_list = jax.random.split(jax.random.key(seed), 7)
    return {
        "projected": gaussian(key_list[0], (SEQS, SEQ, 3, D), 1.0, 6.0, ((0, 4), (1, 32))),
        "short_filter": gaussian(key_list[1], (3, SHORT, D), 0.4, 2.4, (), jnp.float32),
        "residues": gaussian(key_list[2], (GROUPS, POLES), 0.01, 0.06, (), jnp.float32),
        "decay_rates": jnp.clip(jnp.exp(jax.random.uniform(key_list[3], (GROUPS, POLES), jnp.float32, math.log(2.441406286379788e-05), math.log(0.03125))), 2.441406286379788e-05, 0.03125),
        "skip_gain": jnp.clip(1.0 + 0.1 * jax.random.normal(key_list[4], (D,), jnp.float32), 0.5, 1.5),
        "cotangent": gaussian(key_list[5], (SEQS, SEQ, D), 1.0, 6.0, ((0, 4), (1, 32))),
    }


HIGHEST = lax.Precision.HIGHEST

def edge_tables(residues, decay_rates, span):
    offsets = jnp.arange(span).astype(jnp.float32)
    carry_fwd = residues[:, None, :] * jnp.exp(-decay_rates[:, None, :] * (offsets[None, :, None] + 1.0))
    carry_bwd = residues[:, None, :] * jnp.exp(-decay_rates[:, None, :] * (span - offsets)[None, :, None])
    decay_factor = jnp.exp(-decay_rates * span)
    return (carry_fwd, carry_bwd, decay_factor)

def block_tables(residues, decay_rates, block_rows):
    offsets = jnp.arange(block_rows).astype(jnp.float32)
    powers = jnp.exp(-decay_rates[:, :, None] * offsets[None, None, :])
    lag_filter = lax.optimization_barrier(jnp.sum(residues[:, :, None] * powers, axis=1))
    lag_index = (jnp.arange(block_rows)[:, None] - jnp.arange(block_rows)[None, :]).astype(jnp.int32)
    toeplitz = jnp.where(lag_index >= 0, lag_filter[:, jnp.maximum(lag_index, 0)], 0.0)
    carry_fwd, carry_bwd, decay_factor = edge_tables(residues, decay_rates, block_rows)
    return (toeplitz, powers[:, :, ::-1], powers, carry_fwd, carry_bwd, decay_factor)

def forward_local(inputs, tables):
    toeplitz, end_weights, start_weights, carry_fwd, carry_bwd, decay_factor = tables
    local_out = jnp.einsum('gts,bkswg->bktwg', toeplitz, inputs, precision=HIGHEST)
    block_ends = jnp.einsum('gns,bkswg->bknwg', end_weights, inputs, precision=HIGHEST)
    factor = decay_factor.T[:, None, :]

    def advance(carried, block_term):
        return (factor * carried + block_term, carried)
    final_state, entering = lax.scan(advance, jnp.zeros_like(block_ends[:, 0]), jnp.moveaxis(block_ends, 1, 0))
    entering = jnp.moveaxis(entering, 0, 1)
    local_out = local_out + jnp.einsum('gjn,bknwg->bkjwg', carry_fwd, entering, precision=HIGHEST)
    return (local_out, final_state)

def backward_local(grads, tables):
    toeplitz, end_weights, start_weights, carry_fwd, carry_bwd, decay_factor = tables
    local_grad = jnp.einsum('gts,bktwg->bkswg', toeplitz, grads, precision=HIGHEST)
    block_starts = jnp.einsum('gnt,bktwg->bknwg', start_weights, grads, precision=HIGHEST)
    factor = decay_factor.T[:, None, :]

    def advance(carried, block_term):
        return (factor * carried + block_term, carried)
    final_adjoint, following = lax.scan(advance, jnp.zeros_like(block_starts[:, 0]), jnp.moveaxis(block_starts, 1, 0), reverse=True)
    following = jnp.moveaxis(following, 0, 1)
    local_grad = local_grad + jnp.einsum('gsn,bknwg->bkswg', carry_bwd, following, precision=HIGHEST)
    return (local_grad, final_adjoint)

def short_conv(padded, short_filter, count):
    tap_count = short_filter.shape[1]
    total = jnp.zeros((padded.shape[0], count) + padded.shape[2:], jnp.float32)
    for offset in range(tap_count):
        begin = tap_count - 1 - offset
        total = total + short_filter[:, offset, :] * padded[:, begin:begin + count].astype(jnp.float32)
    return total

def short_conv_grad(ahead, short_filter, count):
    tap_count = short_filter.shape[1]
    total = jnp.zeros((ahead.shape[0], count) + ahead.shape[2:], jnp.float32)
    for offset in range(tap_count):
        total = total + short_filter[:, offset, :] * ahead[:, offset:offset + count]
    return total

def filter_grad(grad_mixed, padded, tap_count, count):
    terms = []
    for offset in range(tap_count):
        begin = tap_count - 1 - offset
        terms.append(lax.optimization_barrier(jnp.sum(grad_mixed * padded[:, begin:begin + count].astype(jnp.float32), axis=(0, 1))))
    return jnp.stack(terms, axis=1)

def sequence_pass(projected, cotangent, short_filter, residues, decay_rates, skip_gain):
    length = projected.shape[1]
    channels = projected.shape[3]
    filter_groups = residues.shape[0]
    tap_count = short_filter.shape[1]
    padded = jnp.concatenate([jnp.zeros((1, tap_count - 1) + projected.shape[2:], projected.dtype), projected], axis=1)
    mixed = short_conv(padded, short_filter, length)
    query_part = mixed[:, :, 0]
    key_part = mixed[:, :, 1]
    value_part = mixed[:, :, 2]
    gated = key_part * value_part
    tables = block_tables(residues, decay_rates, BLK)
    block_shape = (1, length // BLK, BLK, channels // filter_groups, filter_groups)
    conv_out, final_state = forward_local(gated.reshape(block_shape), tables)
    filtered = conv_out.reshape(gated.shape) + skip_gain * gated
    output = (query_part * filtered).astype(jnp.bfloat16)
    upstream = cotangent.astype(jnp.float32)
    grad_query = upstream * filtered
    grad_filtered = upstream * query_part
    conv_grad, final_adjoint = backward_local(grad_filtered.reshape(block_shape), tables)
    grad_gated = conv_grad.reshape(gated.shape) + skip_gain * grad_filtered
    grad_mixed = jnp.stack([grad_query, grad_gated * value_part, grad_gated * key_part], axis=2)
    ahead = jnp.concatenate([grad_mixed, jnp.zeros((1, tap_count - 1, 3, channels), jnp.float32)], axis=1)
    grad_projected = short_conv_grad(ahead, short_filter, length).astype(jnp.bfloat16)
    grad_short = filter_grad(grad_mixed, padded, tap_count, length)
    grad_skip = lax.optimization_barrier(jnp.sum(grad_filtered * gated, axis=(0, 1)))
    return (output[0], grad_projected[0], grad_short, grad_skip)

def reference(projected, short_filter, residues, decay_rates, skip_gain, cotangent):

    def single(sequence_pair):
        return sequence_pass(sequence_pair[0][None], sequence_pair[1][None], short_filter, residues, decay_rates, skip_gain)
    outputs, grads_projected, shorts, skips = lax.map(single, (projected, cotangent))
    return (outputs, grads_projected, lax.optimization_barrier(jnp.sum(shorts, axis=0)), lax.optimization_barrier(jnp.sum(skips, axis=0)))
```

```python
import functools
import jax
import jax.numpy as jnp
from jax import lax
from jax.experimental import pallas as pl
from jax.experimental.pallas import tpu as pltpu
from jax.sharding import PartitionSpec as P

MESH = pl.DeviceIdType.MESH
F32 = jnp.float32
ROWS = 128
HALO = 8
EXT = ROWS + HALO
TILES = 8
POLES = 16
TAPS = 7
CHIPS = 16
GRADS = 24


def halo_kernel(proj, cot, prev, nextp, nextc, send_sem, recv_sem):
    dp, me = lax.axis_index("dp"), lax.axis_index("ctx")
    count = lax.axis_size("ctx")
    up, down = lax.rem(me + 1, count), lax.rem(me + count - 1, count)
    barrier = pltpu.get_barrier_semaphore()
    for other in (up, down):
        pl.semaphore_signal(barrier, inc=1, device_id=(dp, other), device_id_type=MESH)
    pl.semaphore_wait(barrier, 2)
    last, first = pl.ds(ROWS - HALO, HALO), pl.ds(0, HALO)
    moves = (
        (proj.at[:, last, :], prev, up),
        (proj.at[:, first, :], nextp, down),
        (cot.at[first, :], nextc, down),
    )
    copies = [
        pltpu.make_async_remote_copy(
            src_ref=source,
            dst_ref=target,
            send_sem=send_sem.at[k],
            recv_sem=recv_sem.at[k],
            device_id=(dp, other),
            device_id_type=MESH,
        )
        for k, (source, target, other) in enumerate(moves)
    ]
    for copy in copies:
        copy.start()
    for copy in copies:
        copy.wait()


def halo(proj, cot):
    channels = proj.shape[2]
    anywhere = pl.BlockSpec(memory_space=pl.ANY)
    return pl.pallas_call(
        halo_kernel,
        name="halo",
        out_shape=(
            jax.ShapeDtypeStruct((3, HALO, channels), proj.dtype),
            jax.ShapeDtypeStruct((3, HALO, channels), proj.dtype),
            jax.ShapeDtypeStruct((HALO, channels), proj.dtype),
        ),
        in_specs=[anywhere, anywhere],
        out_specs=(anywhere, anywhere, anywhere),
        scratch_shapes=[pltpu.SemaphoreType.DMA((3,)), pltpu.SemaphoreType.DMA((3,))],
        compiler_params=pltpu.CompilerParams(collective_id=0, has_side_effects=True),
    )(proj, cot)


def spread(value, target, row):
    count = value.shape[0]
    for lane in range(8):
        target[pl.ds(row * 8 + lane, count, stride=8), :] = value[:, lane * 128 : (lane + 1) * 128]


def spread_rows(source, target, row):
    def body(block, _):
        begin = pl.multiple_of(block * 16, 16)
        spread(source[pl.ds(begin, 16), :].astype(F32), target, row + begin)
        return 0

    lax.fori_loop(0, ROWS // 16, body, 0)


def gather_rows(source, target):
    def body(block, _):
        begin = pl.multiple_of(block * 16, 16)
        for lane in range(8):
            value = source[pl.ds(begin * 8 + lane, 16, stride=8), :]
            target[pl.ds(begin, 16), lane * 128 : (lane + 1) * 128] = value.astype(target.dtype)
        return 0

    lax.fori_loop(0, ROWS // 16, body, 0)


def tiles(ref, row, count):
    return ref[pl.ds(pl.multiple_of(row * 8, 8), count * 8), :].reshape(count, 8, 128)


def put_tiles(ref, row, value):
    ref[pl.ds(pl.multiple_of(row * 8, 8), value.shape[0] * 8), :] = value.reshape(-1, 128)


def total(value):
    parts = [value[n] for n in range(value.shape[0])]
    while len(parts) > 1:
        parts = [a + b for a, b in zip(parts[::2], parts[1::2])]
    return parts[0]


def edge_masks():
    me = lax.axis_index("ctx")
    return (me > 0).astype(F32), (me < lax.axis_size("ctx") - 1).astype(F32)


def first_kernel(proj, cot, prev, nextp, nextc, filt, decay, mixed, states, x, taps, c, g, gf):
    has_prev, has_next = edge_masks()
    for j in range(3):
        spread(prev[j].astype(F32) * has_prev, x.at[j], 0)
        spread_rows(proj.at[j], x.at[j], HALO)
        spread(nextp[j].astype(F32) * has_next, x.at[j], HALO + ROWS)
        spread(filt[j], taps.at[j], 0)
    spread_rows(cot, c, 0)
    spread(nextc[...].astype(F32) * has_next, c, ROWS)

    def conv(block, _):
        t = block * 8
        out = []
        for j in range(3):
            window = tiles(x.at[j], t + 2, 14)
            weight = tiles(taps.at[j], 0, TAPS)
            out.append(sum(weight[i][None] * window[6 - i : 14 - i] for i in range(TAPS)))
            put_tiles(mixed.at[j], t, out[j])
        put_tiles(g, t, out[1] * out[2])
        put_tiles(gf, t, tiles(c, t, 8) * out[0])
        return 0

    lax.fori_loop(0, EXT // 8, conv, 0)
    a = decay[0]

    def step(block, carry):
        s, b = carry
        ahead = tiles(g, block * 8, 8)
        behind = tiles(gf, EXT - 8 - block * 8, 8)
        for u in range(8):
            s = a * s + ahead[u][None]
            b = a * b + behind[7 - u][None]
        return s, b

    zero = jnp.zeros((POLES, 8, 128), F32)
    s, b = lax.fori_loop(0, ROWS // 8, step, (zero, zero))
    states[0] = s
    states[1] = b


def tile_spec(lead, width):
    return pl.BlockSpec(lead + (width,), lambda i: (0,) * len(lead) + (i,))


def first(proj, cot, prev, nextp, nextc, filt, tables):
    whole = pl.BlockSpec((4, POLES, 8, 128), lambda i: (0, 0, 0, 0))
    return pl.pallas_call(
        first_kernel,
        name="first",
        grid=(TILES,),
        out_shape=(
            jax.ShapeDtypeStruct((TILES, 3, EXT * 8, 128), F32),
            jax.ShapeDtypeStruct((2, POLES, TILES * 8, 128), F32),
        ),
        in_specs=[
            tile_spec((3, ROWS), 1024),
            tile_spec((ROWS,), 1024),
            tile_spec((3, HALO), 1024),
            tile_spec((3, HALO), 1024),
            tile_spec((HALO,), 1024),
            tile_spec((3, TAPS), 1024),
            whole,
        ],
        out_specs=(
            pl.BlockSpec((None, 3, EXT * 8, 128), lambda i: (i, 0, 0, 0)),
            pl.BlockSpec((2, POLES, 8, 128), lambda i: (0, 0, i, 0)),
        ),
        scratch_shapes=[
            pltpu.VMEM((3, (EXT + HALO) * 8, 128), F32),
            pltpu.VMEM((3, TAPS * 8, 128), F32),
            pltpu.VMEM((EXT * 8, 128), F32),
            pltpu.VMEM((EXT * 8, 128), F32),
            pltpu.VMEM((EXT * 8, 128), F32),
        ],
        compiler_params=pltpu.CompilerParams(vmem_limit_bytes=48 << 20),
    )(proj, cot, prev, nextp, nextc, filt, tables)


def place():
    dp, me = lax.axis_index("dp"), lax.axis_index("ctx")
    return dp, lax.div(me, 2), lax.rem(me, 2)


def remote(source, target, send_sem, recv_sem, dp, chip, core):
    return pltpu.make_async_remote_copy(
        src_ref=source,
        dst_ref=target,
        send_sem=send_sem,
        recv_sem=recv_sem,
        device_id=(dp, chip * 2 + core),
        device_id_type=MESH,
    )


def greet(dp, chip, core, lines):
    barrier = pltpu.get_barrier_semaphore()

    def plane(offset, _):
        other = lax.rem(chip + offset, CHIPS)
        pl.semaphore_signal(barrier, inc=1, device_id=(dp, other * 2 + core), device_id_type=MESH)
        return 0

    lax.fori_loop(1, CHIPS, plane, 0)
    pl.semaphore_signal(barrier, inc=1, device_id=(dp, chip * 2 + 1 - core), device_id_type=MESH)
    for offset in range(1, lines):
        other = lax.rem(dp + offset, lines)
        pl.semaphore_signal(barrier, inc=1, device_id=(other, chip * 2 + core), device_id_type=MESH)
    pl.semaphore_wait(barrier, CHIPS + lines - 1)


def exchange(source, target, send_sem, recv_sem, dp, chip, core, spread_source=True):
    def copy(other, slot):
        return remote(
            source.at[other] if spread_source else source,
            target.at[slot],
            send_sem.at[other],
            recv_sem.at[slot],
            dp,
            other,
            core,
        )

    def start(offset, _):
        copy(lax.rem(chip + offset, CHIPS), chip).start()
        return 0

    lax.fori_loop(1, CHIPS, start, 0)
    target[chip] = source[chip] if spread_source else source[...]

    def wait(offset, _):
        other = lax.rem(chip + CHIPS - offset, CHIPS)
        copy(other, other).wait_recv()
        return 0

    lax.fori_loop(1, CHIPS, wait, 0)

    def sent(offset, _):
        copy(lax.rem(chip + offset, CHIPS), chip).wait_send()
        return 0

    lax.fori_loop(1, CHIPS, sent, 0)


def scan_kernel(local, tables, out, partner, ends, came, back, entering, give, land, pair_send, pair_recv, send1, recv1, send2, recv2):
    dp, chip, core = place()
    half = TILES * 4
    mine, theirs = pl.ds(core * half, half), pl.ds((1 - core) * half, half)
    greet(dp, chip, core, 1)
    copy = remote(local.at[:, :, theirs, :], partner, pair_send.at[0], pair_recv.at[0], dp, chip, 1 - core)
    copy.start()
    copy.wait()
    low = core == 0

    def merge(n, _):
        d = tables[2, n][None]
        own = local[:, n, mine, :].reshape(2, TILES // 2, 8, 128)
        other = partner[:, n].reshape(2, TILES // 2, 8, 128)
        lo, hi = jnp.where(low, own, other), jnp.where(low, other, own)
        ends[n, 0] = (d * lo[0] + hi[0]).reshape(half, 128)
        ends[n, 1] = (lo[1] + d * hi[1]).reshape(half, 128)
        return 0

    lax.fori_loop(0, POLES, merge, 0)
    exchange(ends, came, send1, recv1, dp, chip, core)
    d2 = tables[3, chip][None]

    def ahead(q, s):
        back[q, 0] = s.reshape(half, 128)
        return d2 * s + came[q, 0].reshape(TILES // 2, 8, 128)

    def behind(k, s):
        q = CHIPS - 1 - k
        back[q, 1] = s.reshape(half, 128)
        return d2 * s + came[q, 1].reshape(TILES // 2, 8, 128)

    zero = jnp.zeros((TILES // 2, 8, 128), F32)
    lax.fori_loop(0, CHIPS, ahead, zero)
    lax.fori_loop(0, CHIPS, behind, zero)
    exchange(back, entering, send2, recv2, dp, chip, core)

    def split(n, _):
        d = tables[2, n][None]
        own = local[:, n, mine, :].reshape(2, TILES // 2, 8, 128)
        other = partner[:, n].reshape(2, TILES // 2, 8, 128)
        lo, hi = jnp.where(low, own, other), jnp.where(low, other, own)
        e = entering[n].reshape(2, TILES // 2, 8, 128)
        fwd_lo, fwd_hi = e[0], d * e[0] + lo[0]
        bwd_lo, bwd_hi = d * e[1] + hi[1], e[1]
        out[0, n, mine, :] = jnp.where(low, fwd_lo, fwd_hi).reshape(half, 128)
        out[1, n, mine, :] = jnp.where(low, bwd_lo, bwd_hi).reshape(half, 128)
        give[0, n] = jnp.where(low, fwd_hi, fwd_lo).reshape(half, 128)
        give[1, n] = jnp.where(low, bwd_hi, bwd_lo).reshape(half, 128)
        return 0

    lax.fori_loop(0, POLES, split, 0)
    copy = remote(give, land, pair_send.at[1], pair_recv.at[1], dp, chip, 1 - core)
    copy.start()
    copy.wait()
    out[:, :, theirs, :] = land[...]


def scan_states(states, tables):
    half = TILES * 4
    vmem = pl.BlockSpec(memory_space=pltpu.VMEM)
    pair = pltpu.VMEM((2, POLES, half, 128), F32)
    slots = pltpu.VMEM((CHIPS, 2, half, 128), F32)
    many = pltpu.SemaphoreType.DMA((CHIPS,))
    return pl.pallas_call(
        scan_kernel,
        name="scan_states",
        out_shape=jax.ShapeDtypeStruct(states.shape, F32),
        in_specs=[vmem, vmem],
        out_specs=vmem,
        scratch_shapes=[pair, slots, slots, slots, slots, pair, pair]
        + [pltpu.SemaphoreType.DMA((2,)), pltpu.SemaphoreType.DMA((2,)), many, many, many, many],
        compiler_params=pltpu.CompilerParams(
            collective_id=1, has_side_effects=True, vmem_limit_bytes=32 << 20
        ),
    )(states, tables)


def second_kernel(proj, cot, prev, nextc, filt, skip, tables, mixed, states, output, grad_proj, grads, x, taps, c, gm, o):
    has_prev, has_next = edge_masks()
    for j in range(3):
        spread(prev[j].astype(F32) * has_prev, x.at[j], 0)
        spread_rows(proj.at[j], x.at[j], HALO)
        spread(filt[j], taps.at[j], 0)
    spread_rows(cot, c, 0)
    spread(nextc[...].astype(F32) * has_next, c, ROWS)
    gain = skip[...]

    def step(block, carry):
        s, b = carry
        begin, end = block * 4, EXT - 4 - block * 4
        a, r = tables[0], tables[1]
        k0, v0 = tiles(mixed.at[1], begin, 4), tiles(mixed.at[2], begin, 4)
        g = k0 * v0
        gf = tiles(c, end, 4) * tiles(mixed.at[0], end, 4)
        fwd, bwd = [], []
        for u in range(4):
            s = a * s + g[u][None]
            b = a * b + gf[3 - u][None]
            fwd.append(total(r * s))
            bwd.append(total(r * b))
        filtered = jnp.stack(fwd) + gain[None] * g
        grad_gated = jnp.stack(bwd[::-1]) + gain[None] * gf
        put_tiles(o, begin, tiles(mixed.at[0], begin, 4) * filtered)
        put_tiles(gm.at[0], begin, tiles(c, begin, 4) * filtered)
        put_tiles(gm.at[1], end, grad_gated * tiles(mixed.at[2], end, 4))
        put_tiles(gm.at[2], end, grad_gated * tiles(mixed.at[1], end, 4))
        return s, b

    lax.fori_loop(0, EXT // 4, step, (states[0], states[1]))
    gather_rows(o, output)

    def skip_sum(block, acc):
        t = block * 8
        terms = tiles(c, t, 8) * tiles(mixed.at[0], t, 8) * (tiles(mixed.at[1], t, 8) * tiles(mixed.at[2], t, 8))
        return acc + total(terms)

    grads[pl.ds(21 * 8, 8), :] = lax.fori_loop(0, ROWS // 8, skip_sum, jnp.zeros((8, 128), F32))
    grads[pl.ds(22 * 8, 16), :] = jnp.zeros((16, 128), F32)
    for j in range(3):
        weight = tiles(taps.at[j], 0, TAPS)

        def conv(block, acc):
            t = block * 8
            ahead = tiles(gm.at[j], t, 14)
            window = tiles(x.at[j], t + 2, 14)
            put_tiles(o, t, sum(weight[i][None] * ahead[i : i + 8] for i in range(TAPS)))
            return tuple(acc[i] + total(ahead[:8] * window[6 - i : 14 - i]) for i in range(TAPS))

        acc = lax.fori_loop(0, ROWS // 8, conv, (jnp.zeros((8, 128), F32),) * TAPS)
        for i in range(TAPS):
            grads[pl.ds((j * TAPS + i) * 8, 8), :] = acc[i]
        gather_rows(o, grad_proj.at[j])


def second(proj, cot, prev, nextc, filt, skip, tables, mixed, states):
    return pl.pallas_call(
        second_kernel,
        name="second",
        grid=(TILES,),
        out_shape=(
            jax.ShapeDtypeStruct((ROWS, TILES * 1024), jnp.bfloat16),
            jax.ShapeDtypeStruct((3, ROWS, TILES * 1024), jnp.bfloat16),
            jax.ShapeDtypeStruct((TILES, GRADS * 8, 128), F32),
        ),
        in_specs=[
            tile_spec((3, ROWS), 1024),
            tile_spec((ROWS,), 1024),
            tile_spec((3, HALO), 1024),
            tile_spec((HALO,), 1024),
            tile_spec((3, TAPS), 1024),
            pl.BlockSpec((None, 8, 128), lambda i: (i, 0, 0)),
            pl.BlockSpec((4, POLES, 8, 128), lambda i: (0, 0, 0, 0)),
            pl.BlockSpec((None, 3, EXT * 8, 128), lambda i: (i, 0, 0, 0)),
            pl.BlockSpec((2, POLES, 8, 128), lambda i: (0, 0, i, 0)),
        ],
        out_specs=(
            tile_spec((ROWS,), 1024),
            tile_spec((3, ROWS), 1024),
            pl.BlockSpec((None, GRADS * 8, 128), lambda i: (i, 0, 0)),
        ),
        scratch_shapes=[
            pltpu.VMEM((3, (EXT + HALO) * 8, 128), F32),
            pltpu.VMEM((3, TAPS * 8, 128), F32),
            pltpu.VMEM((EXT * 8, 128), F32),
            pltpu.VMEM((3, EXT * 8, 128), F32),
            pltpu.VMEM((EXT * 8, 128), F32),
        ],
        compiler_params=pltpu.CompilerParams(vmem_limit_bytes=48 << 20),
    )(proj, cot, prev, nextc, filt, skip, tables, mixed, states)


def sum_kernel(grads, out, partner, slices, came, part, lines, around, land, pair_send, pair_recv, send1, recv1, line_send, line_recv, send2, recv2):
    dp, chip, core = place()
    depth = lax.axis_size("dp")
    half = TILES // 2
    mine, theirs = pl.ds(core * half, half), pl.ds((1 - core) * half, half)
    greet(dp, chip, core, depth)
    copy = remote(grads.at[theirs], partner, pair_send.at[0], pair_recv.at[0], dp, chip, 1 - core)
    copy.start()
    copy.wait()
    whole = grads[mine] + partner[...]
    slices[...] = whole.reshape(slices.shape)
    exchange(slices, came, send1, recv1, dp, chip, core)
    acc = came[0]
    for q in range(1, CHIPS):
        acc = acc + came[q]
    part[...] = acc

    def line(other, slot):
        return pltpu.make_async_remote_copy(
            src_ref=part,
            dst_ref=lines.at[slot],
            send_sem=line_send.at[other],
            recv_sem=line_recv.at[slot],
            device_id=(other, chip * 2 + core),
            device_id_type=MESH,
        )

    for offset in range(1, depth):
        line(lax.rem(dp + offset, depth), dp).start()
    lines[dp] = acc
    for offset in range(1, depth):
        other = lax.rem(dp + depth - offset, depth)
        line(other, other).wait_recv()
    for offset in range(1, depth):
        line(lax.rem(dp + offset, depth), dp).wait_send()
    acc = lines[0]
    for q in range(1, depth):
        acc = acc + lines[q]
    part[...] = acc
    exchange(part, around, send2, recv2, dp, chip, core, spread_source=False)
    copy = remote(around, land, pair_send.at[1], pair_recv.at[1], dp, chip, 1 - core)
    copy.start()
    out[mine] = around[...].reshape(whole.shape)
    copy.wait()
    out[theirs] = land[...].reshape(whole.shape)


def sum_grads(grads):
    vmem = pl.BlockSpec(memory_space=pltpu.VMEM)
    piece = TILES // 2 * GRADS * 8 // CHIPS
    slots = pltpu.VMEM((CHIPS, piece, 128), F32)
    many = pltpu.SemaphoreType.DMA((CHIPS,))
    few = pltpu.SemaphoreType.DMA((4,))
    two = pltpu.SemaphoreType.DMA((2,))
    return pl.pallas_call(
        sum_kernel,
        name="sum_grads",
        out_shape=jax.ShapeDtypeStruct(grads.shape, F32),
        in_specs=[vmem],
        out_specs=vmem,
        scratch_shapes=[
            pltpu.VMEM((TILES // 2, GRADS * 8, 128), F32),
            slots,
            slots,
            pltpu.VMEM((piece, 128), F32),
            pltpu.VMEM((4, piece, 128), F32),
            slots,
            slots,
            two,
            two,
            many,
            many,
            few,
            few,
            many,
            many,
        ],
        compiler_params=pltpu.CompilerParams(
            collective_id=2, has_side_effects=True, vmem_limit_bytes=32 << 20
        ),
    )(grads)


def coefficient_tables(residues, decay_rates):
    rates, weights = decay_rates.T, residues.T
    table = jnp.stack(
        [jnp.exp(-rates), weights, jnp.exp(-rates * ROWS), jnp.exp(-rates * (2 * ROWS))]
    ).reshape(4, POLES, 4, 128)
    return jnp.concatenate([table, table], axis=2)


def local(projected, short_filter, residues, decay_rates, skip_gain, cotangent):
    proj = jnp.transpose(projected[0], (1, 0, 2))
    cot = cotangent[0]
    channels = proj.shape[2]
    tables = coefficient_tables(residues, decay_rates)
    prev, nextp, nextc = halo(proj, cot)
    mixed, states = first(proj, cot, prev, nextp, nextc, short_filter, tables)
    states = scan_states(states, tables)
    skip = skip_gain.reshape(TILES, 8, 128)
    output, grad_proj, grads = second(proj, cot, prev, nextc, short_filter, skip, tables, mixed, states)
    sums = sum_grads(grads).reshape(TILES, GRADS, 1024).transpose(1, 0, 2).reshape(GRADS, channels)
    return (
        output[None],
        jnp.transpose(grad_proj, (1, 0, 2))[None],
        sums[:21].reshape(3, TAPS, channels),
        sums[21],
    )


def solution(mesh):
    placed = (P("dp", "ctx", None, None), P(), P(), P(), P(), P("dp", "ctx", None))
    return jax.shard_map(
        local,
        mesh=mesh,
        in_specs=placed,
        out_specs=(P("dp", "ctx", None), P("dp", "ctx", None, None), P(), P()),
        check_vma=False,
    )
```

```python
import jax
import jax.numpy as jnp
from jax import lax
from jax.experimental import pallas as pl
from jax.experimental.pallas import tpu as pltpu
from jax.sharding import PartitionSpec as P

MESH = pl.DeviceIdType.MESH
F32 = jnp.float32
BF16 = jnp.bfloat16
ROWS = 128
HALO = 8
EXT = ROWS + HALO
TILES = 8
WIDE = 1024
POLES = 16
TAPS = 7
CHIPS = 16
LINES = 4
GRADS = 24
GROUPS = 4
SUMS = 2
PIECE = TILES // SUMS // 2 * GRADS * 8 // CHIPS


def spread(value, target, row):
    count = value.shape[0]
    for lane in range(8):
        target[pl.ds(row * 8 + lane, count, stride=8), :] = value[:, lane * 128 : (lane + 1) * 128]


def spread_rows(source, target, row):
    def body(block, _):
        begin = pl.multiple_of(block * 16, 16)
        spread(source[pl.ds(begin, 16), :].astype(F32), target, row + begin)
        return 0

    lax.fori_loop(0, ROWS // 16, body, 0)


def gather_rows(source, target):
    def body(block, _):
        begin = pl.multiple_of(block * 16, 16)
        for lane in range(8):
            value = source[pl.ds(begin * 8 + lane, 16, stride=8), :]
            target[pl.ds(begin, 16), lane * 128 : (lane + 1) * 128] = value.astype(target.dtype)
        return 0

    lax.fori_loop(0, ROWS // 16, body, 0)


def tiles(ref, row, count):
    return ref[pl.ds(pl.multiple_of(row * 8, 8), count * 8), :].reshape(count, 8, 128)


def put_tiles(ref, row, value):
    ref[pl.ds(pl.multiple_of(row * 8, 8), value.shape[0] * 8), :] = value.reshape(-1, 128)


def total(value):
    while value.shape[0] > 1:
        half = value.shape[0] // 2
        value = value[:half] + value[half:]
    return value[0]


def kernel(
    proj, cot, filt, skip, rates, weights,
    output, grad_proj, grad_short, grad_skip,
    x, mix, c, yf, yb, ins, outs, prev, nextp, nextc, taps, tables,
    st, st_pair, st_ends, st_came, st_back, st_enter, st_give, st_land, ea,
    gr, gr_pair, gr_cut, gr_came, gr_part, gr_whole, gr_lines, gr_around, gr_land,
    in_sem, out_sem, halo_send, halo_recv,
    st_ps, st_pr, st_s1, st_r1, st_s2, st_r2, st_ls, st_lr,
    gr_ps, gr_pr, gr_s1, gr_r1, gr_s2, gr_r2, gr_ls, gr_lr,
):
    dp, me = lax.axis_index("dp"), lax.axis_index("ctx")
    count = 2 * CHIPS
    chip, core = lax.div(me, 2), lax.rem(me, 2)
    low = core == 0
    up, down = lax.rem(me + 1, count), lax.rem(me + count - 1, count)
    has_prev = (me > 0).astype(F32)
    has_next = (me < count - 1).astype(F32)

    def remote(source, target, send_sem, recv_sem, line, ctx):
        return pltpu.make_async_remote_copy(
            src_ref=source,
            dst_ref=target,
            send_sem=send_sem,
            recv_sem=recv_sem,
            device_id=(line, ctx),
            device_id_type=MESH,
        )

    barrier = pltpu.get_barrier_semaphore()

    def greet(offset, _):
        other = lax.rem(chip + offset, CHIPS) * 2 + core
        pl.semaphore_signal(barrier, inc=1, device_id=(dp, other), device_id_type=MESH)
        return 0

    lax.fori_loop(1, CHIPS, greet, 0)
    for other in (chip * 2 + 1 - core, up, down):
        pl.semaphore_signal(barrier, inc=1, device_id=(dp, other), device_id_type=MESH)
    for offset in range(1, LINES):
        line = lax.rem(dp + offset, LINES)
        pl.semaphore_signal(barrier, inc=1, device_id=(line, me), device_id_type=MESH)

    def fetch(tile):
        slot = lax.rem(tile, 2)
        lanes = pl.ds(pl.multiple_of(tile * WIDE, WIDE), WIDE)
        return (
            pltpu.make_async_copy(proj.at[:, :, lanes], ins.at[slot, pl.ds(0, 3)], in_sem.at[slot, 0]),
            pltpu.make_async_copy(cot.at[:, lanes], ins.at[slot, 3], in_sem.at[slot, 1]),
        )

    for tile in range(2):
        for copy in fetch(tile):
            copy.start()

    for quarter in range(4):
        lanes = slice(quarter * 128, (quarter + 1) * 128)
        rate = rates[:, lanes]
        rows = (jnp.exp(-rate), weights[:, lanes], jnp.exp(-rate * ROWS), jnp.exp(-rate * (2 * ROWS)))
        for k in range(4):
            for again in (0, 4):
                tables[k, pl.ds(quarter + again, POLES, stride=8), :] = rows[k]

    def table(k):
        return tables[k].reshape(POLES, 8, 128)

    def short_filter(tile, block):
        t = block * 8
        for j in range(3):
            window = tiles(x.at[tile, j], t + 2, 14)
            weight = tiles(taps.at[tile, j], 0, TAPS)
            part = weight[0][None] * window[6:14]
            for i in range(1, TAPS):
                part = part + weight[i][None] * window[6 - i : 14 - i]
            put_tiles(mix.at[tile, j], t, part)

    def load_tile(tile):
        slot = lax.rem(tile, 2)
        for copy in fetch(tile):
            copy.wait()
        lanes = pl.ds(pl.multiple_of(tile * WIDE, WIDE), WIDE)
        for j in range(3):
            spread_rows(ins.at[slot, j], x.at[tile, j], HALO)
            spread(filt[j, :, lanes], taps.at[tile, j], 0)
        spread_rows(ins.at[slot, 3], c.at[tile], 0)

        @pl.when(tile < TILES - 2)
        def _():
            for copy in fetch(tile + 2):
                copy.start()

        def inner(block, _):
            short_filter(tile, block)
            return 0

        lax.fori_loop(1, ROWS // 8, inner, 0)

    pl.semaphore_wait(barrier, CHIPS - 1 + 3 + LINES - 1)
    last, first = pl.ds(ROWS - HALO, HALO), pl.ds(0, HALO)
    halo = (
        remote(proj.at[:, last, :], prev, halo_send.at[0], halo_recv.at[0], dp, up),
        remote(proj.at[:, first, :], nextp, halo_send.at[1], halo_recv.at[1], dp, down),
        remote(cot.at[first, :], nextc, halo_send.at[2], halo_recv.at[2], dp, down),
    )
    for copy in halo:
        copy.start()

    def load_loop(tile, _):
        load_tile(tile)
        return 0

    lax.fori_loop(0, TILES, load_loop, 0)
    for copy in halo:
        copy.wait()

    def plane_send(source, target, send_sem, recv_sem):
        def start(offset, _):
            other = lax.rem(chip + offset, CHIPS)
            remote(source(other), target.at[chip], send_sem, recv_sem, dp, other * 2 + core).start()
            return 0

        lax.fori_loop(1, CHIPS, start, 0)
        target[chip] = source(chip)[...]

    def plane_wait(target, send_sem, recv_sem):
        most = target.at[pl.ds(0, CHIPS - 1)]
        copy = remote(most, most, send_sem, recv_sem, dp, me)
        copy.wait_recv()
        copy.wait_send()

    pair = chip * 2 + 1 - core

    def mine(group):
        return pl.ds(pl.multiple_of((group * 2 + core) * 8, 8), 8)

    def theirs(group):
        return pl.ds(pl.multiple_of((group * 2 + 1 - core) * 8, 8), 8)

    def st_pair_copy(g):
        return remote(st.at[:, :, theirs(g), :], st_pair.at[g], st_ps.at[g], st_pr.at[g], dp, pair)

    def st_back_copy(g):
        return remote(st_give.at[g], st_land.at[g], st_ls.at[g], st_lr.at[g], dp, pair)

    def low_high(g):
        own, other = st[:, :, mine(g), :], st_pair[g]
        return jnp.where(low, own, other), jnp.where(low, other, own)

    def st_1(g):
        st_pair_copy(g).start()

    def st_2(g):
        st_pair_copy(g).wait()
        lo, hi = low_high(g)
        d = table(2)
        st_ends[g, :, 0] = d * lo[0] + hi[0]
        st_ends[g, :, 1] = lo[1] + d * hi[1]
        plane_send(lambda q: st_ends.at[g, q], st_came.at[g], st_s1.at[g], st_r1.at[g])

    def st_3(g):
        plane_wait(st_came.at[g], st_s1.at[g], st_r1.at[g])
        d2 = tables[3, pl.ds(pl.multiple_of(chip * 8, 8), 8), :]
        s = jnp.zeros((8, 128), F32)
        for q in range(CHIPS):
            st_back[g, q, 0] = s
            s = d2 * s + st_came[g, q, 0]
        s = jnp.zeros((8, 128), F32)
        for q in reversed(range(CHIPS)):
            st_back[g, q, 1] = s
            s = d2 * s + st_came[g, q, 1]
        plane_send(lambda q: st_back.at[g, q], st_enter.at[g], st_s2.at[g], st_r2.at[g])

    def st_4(g):
        plane_wait(st_enter.at[g], st_s2.at[g], st_r2.at[g])
        lo, hi = low_high(g)
        d = table(2)
        fwd, bwd = st_enter[g, :, 0], st_enter[g, :, 1]
        fwd_hi, bwd_lo = d * fwd + lo[0], d * bwd + hi[1]
        ea[0, :, mine(g), :] = jnp.where(low, fwd, fwd_hi)
        ea[1, :, mine(g), :] = jnp.where(low, bwd_lo, bwd)
        st_give[g, 0] = jnp.where(low, fwd_hi, fwd)
        st_give[g, 1] = jnp.where(low, bwd, bwd_lo)
        st_back_copy(g).start()

    def st_5(g):
        st_back_copy(g).wait()
        ea[:, :, theirs(g), :] = st_land[g]

    def st_hooks(slot):
        step = lax.div(slot, 2)
        even = lax.rem(slot, 2) == 0

        @pl.when(jnp.logical_and(even, jnp.logical_and(step >= 3, step < GROUPS + 3)))
        def _():
            st_4(step - 3)

        @pl.when(jnp.logical_and(even, jnp.logical_and(step >= 2, step < GROUPS + 2)))
        def _():
            st_3(step - 2)

        @pl.when(jnp.logical_and(even, jnp.logical_and(step >= 1, step < GROUPS + 1)))
        def _():
            st_2(step - 1)

    def local_scan(tile):
        q, k, v = mix.at[tile, 0], mix.at[tile, 1], mix.at[tile, 2]

        def step(block, carry):
            s, b = carry
            begin, end = block * 4, EXT - 4 - block * 4
            a, r = table(0), table(1)
            g = tiles(k, begin, 4) * tiles(v, begin, 4)
            gf = tiles(c.at[tile], end, 4) * tiles(q, end, 4)
            fwd, bwd = [], []
            for u in range(4):
                s = a * s + g[u][None]
                b = a * b + gf[3 - u][None]
                fwd.append(total(r * s))
                bwd.append(total(r * b))
            put_tiles(yf.at[tile], begin, jnp.stack(fwd))
            put_tiles(yb.at[tile], end, jnp.stack(bwd[::-1]))
            return s, b

        zero = jnp.zeros((POLES, 8, 128), F32)
        s, b = lax.fori_loop(0, ROWS // 4, step, (zero, zero))
        rows = pl.ds(pl.multiple_of(tile * 8, 8), 8)
        st[0, :, rows, :] = s
        st[1, :, rows, :] = b
        lax.fori_loop(ROWS // 4, EXT // 4, step, (s, b))

    def scan_loop(tile, _):
        lanes = pl.ds(pl.multiple_of(tile * WIDE, WIDE), WIDE)
        for j in range(3):
            spread(prev[j, :, lanes].astype(F32) * has_prev, x.at[tile, j], 0)
            spread(nextp[j, :, lanes].astype(F32) * has_next, x.at[tile, j], HALO + ROWS)
        spread(nextc[:, lanes].astype(F32) * has_next, c.at[tile], ROWS)

        def edge(block, _):
            short_filter(tile, block * (ROWS // 8))
            return 0

        lax.fori_loop(0, 2, edge, 0)
        local_scan(tile)

        @pl.when(lax.rem(tile, 2) == 1)
        def _():
            st_1(lax.div(tile, 2))

        st_hooks(tile)
        return 0

    lax.fori_loop(0, TILES, scan_loop, 0)

    half = TILES // SUMS // 2

    def own(h):
        return pl.ds(h * 2 * half + core * half, half)

    def others(h):
        return pl.ds(h * 2 * half + (1 - core) * half, half)

    def gr_pair_copy(h):
        return remote(gr.at[others(h)], gr_pair.at[h], gr_ps.at[h, 0], gr_pr.at[h, 0], dp, pair)

    def gr_back_copy(h):
        return remote(gr_around.at[h], gr_land.at[h], gr_ps.at[h, 1], gr_pr.at[h, 1], dp, pair)

    def gr_1(h):
        gr_pair_copy(h).start()

    def gr_2(h):
        gr_pair_copy(h).wait()
        gr_cut[h] = (gr[own(h)] + gr_pair[h]).reshape(CHIPS, PIECE, 128)
        plane_send(lambda q: gr_cut.at[h, q], gr_came.at[h], gr_s1.at[h], gr_r1.at[h])

    def line_copy(h, other, slot):
        return remote(gr_part.at[h], gr_lines.at[h, slot], gr_ls.at[h, other], gr_lr.at[h, slot], other, me)

    def gr_3(h):
        plane_wait(gr_came.at[h], gr_s1.at[h], gr_r1.at[h])
        part = gr_came[h, 0]
        for q in range(1, CHIPS):
            part = part + gr_came[h, q]
        gr_part[h] = part
        gr_lines[h, dp] = part
        for offset in range(1, LINES):
            line_copy(h, lax.rem(dp + offset, LINES), dp).start()

    def gr_4(h):
        for offset in range(1, LINES):
            other = lax.rem(dp + offset, LINES)
            line_copy(h, other, other).wait_recv()
            line_copy(h, other, dp).wait_send()
        part = gr_lines[h, 0]
        for q in range(1, LINES):
            part = part + gr_lines[h, q]
        gr_whole[h] = part
        plane_send(lambda q: gr_whole.at[h], gr_around.at[h], gr_s2.at[h], gr_r2.at[h])

    def gr_5(h):
        plane_wait(gr_around.at[h], gr_s2.at[h], gr_r2.at[h])
        gr_back_copy(h).start()

    def gr_6(h):
        gr_back_copy(h).wait()
        gr[own(h)] = gr_around[h].reshape(half, GRADS * 8, 128)
        gr[others(h)] = gr_land[h].reshape(half, GRADS * 8, 128)

    def correct(tile):
        q, k, v = mix.at[tile, 0], mix.at[tile, 1], mix.at[tile, 2]
        rows = pl.ds(pl.multiple_of(tile * 8, 8), 8)
        gain = skip[rows, :][None]

        def ahead(block, carry):
            e, acc = carry
            t = block * 4
            a = table(0)
            more = []
            for _ in range(4):
                e = a * e
                more.append(total(e))
            g = tiles(k, t, 4) * tiles(v, t, 4)
            query, upstream = tiles(q, t, 4), tiles(c.at[tile], t, 4)
            filtered = tiles(yf.at[tile], t, 4) + jnp.stack(more) + gain * g
            gf = upstream * query
            put_tiles(yf.at[tile], t, query * filtered)
            put_tiles(c.at[tile], t, upstream * filtered)
            put_tiles(q, t, gf)
            return e, acc + total(gf * g)

        start = table(1) * ea[0, :, rows, :]
        e, acc = lax.fori_loop(0, ROWS // 4, ahead, (start, jnp.zeros((8, 128), F32)))
        gr[tile, pl.ds(21 * 8, 8), :] = acc
        gr[tile, pl.ds(22 * 8, 16), :] = jnp.zeros((16, 128), F32)
        lax.fori_loop(ROWS // 4, EXT // 4, ahead, (e, acc))

        def behind(block, e):
            t = EXT - 4 - block * 4
            a = table(0)
            more = []
            for _ in range(4):
                e = a * e
                more.append(total(e))
            grad_gated = tiles(yb.at[tile], t, 4) + jnp.stack(more[::-1]) + gain * tiles(q, t, 4)
            key, value = tiles(k, t, 4), tiles(v, t, 4)
            put_tiles(k, t, grad_gated * value)
            put_tiles(v, t, grad_gated * key)
            return e

        lax.fori_loop(0, EXT // 4, behind, table(1) * ea[1, :, rows, :])

    def mixed_grad(tile, j):
        return c.at[tile] if j == 0 else mix.at[tile, j]

    def tap_grads(tile):
        for j in range(3):

            def body(block, acc):
                t = block * 8
                grad = tiles(mixed_grad(tile, j), t, 8)
                window = tiles(x.at[tile, j], t + 2, 14)
                return tuple(acc[i] + total(grad * window[6 - i : 14 - i]) for i in range(TAPS))

            acc = lax.fori_loop(0, ROWS // 8, body, (jnp.zeros((8, 128), F32),) * TAPS)
            for i in range(TAPS):
                gr[tile, pl.ds((j * TAPS + i) * 8, 8), :] = acc[i]

    def post_loop(tile, _):
        @pl.when(lax.rem(tile, 2) == 0)
        def _():
            st_5(lax.div(tile, 2))

        correct(tile)
        tap_grads(tile)
        st_hooks(tile + TILES)

        @pl.when(tile == 3)
        def _():
            gr_1(0)

        @pl.when(tile == 4)
        def _():
            gr_2(0)

        @pl.when(tile == 6)
        def _():
            gr_3(0)

        return 0

    lax.fori_loop(0, TILES, post_loop, 0)
    gr_1(1)

    def leave(tile):
        slot = lax.rem(tile, 2)
        lanes = pl.ds(pl.multiple_of(tile * WIDE, WIDE), WIDE)
        return (
            pltpu.make_async_copy(outs.at[slot, pl.ds(0, 3)], grad_proj.at[:, :, lanes], out_sem.at[slot, 0]),
            pltpu.make_async_copy(outs.at[slot, 3], output.at[:, lanes], out_sem.at[slot, 1]),
        )

    def out_loop(tile, _):
        slot = lax.rem(tile, 2)

        @pl.when(tile >= 2)
        def _():
            for copy in leave(tile - 2):
                copy.wait()

        for j in range(3):

            def body(block, _):
                t = block * 8
                ahead = tiles(mixed_grad(tile, j), t, 14)
                weight = tiles(taps.at[tile, j], 0, TAPS)
                part = weight[0][None] * ahead[0:8]
                for i in range(1, TAPS):
                    part = part + weight[i][None] * ahead[i : i + 8]
                put_tiles(x.at[tile, j], t, part)
                return 0

            lax.fori_loop(0, ROWS // 8, body, 0)
            gather_rows(x.at[tile, j], outs.at[slot, j])
        gather_rows(yf.at[tile], outs.at[slot, 3])
        for copy in leave(tile):
            copy.start()

        @pl.when(tile == 0)
        def _():
            gr_4(0)
            gr_2(1)

        @pl.when(tile == 4)
        def _():
            gr_5(0)
            gr_3(1)

        @pl.when(tile == 6)
        def _():
            gr_6(0)

        return 0

    lax.fori_loop(0, TILES, out_loop, 0)
    gr_4(1)
    gr_5(1)
    for tile in range(TILES - 2, TILES):
        for copy in leave(tile):
            copy.wait()
    gr_6(1)
    for tile in range(TILES):
        grad_skip[tile * 8 : tile * 8 + 8, :] = gr[tile, 21 * 8 : 22 * 8, :]
        for j in range(3):
            for lane in range(8):
                value = gr[tile, pl.ds(j * TAPS * 8 + lane, TAPS, stride=8), :]
                begin = tile * WIDE + lane * 128
                grad_short[j, :, begin : begin + 128] = value


def whole(proj, cot, filt, skip, rates, weights):
    channels = proj.shape[2]
    anywhere = pl.BlockSpec(memory_space=pl.ANY)
    vmem = pl.BlockSpec(memory_space=pltpu.VMEM)

    def buffer(*shape, kind=F32):
        return pltpu.VMEM(shape, kind)

    def dma(*shape):
        return pltpu.SemaphoreType.DMA(shape)

    return pl.pallas_call(
        kernel,
        name="hyena",
        out_shape=(
            jax.ShapeDtypeStruct((ROWS, channels), BF16),
            jax.ShapeDtypeStruct((3, ROWS, channels), BF16),
            jax.ShapeDtypeStruct((3, TAPS, channels), F32),
            jax.ShapeDtypeStruct((TILES * 8, 128), F32),
        ),
        in_specs=[anywhere, anywhere, vmem, vmem, vmem, vmem],
        out_specs=(anywhere, anywhere, vmem, vmem),
        scratch_shapes=[
            buffer(TILES, 3, (EXT + HALO) * 8, 128),
            buffer(TILES, 3, EXT * 8, 128),
            buffer(TILES, EXT * 8, 128),
            buffer(TILES, EXT * 8, 128),
            buffer(TILES, EXT * 8, 128),
            buffer(2, 4, ROWS, WIDE, kind=BF16),
            buffer(2, 4, ROWS, WIDE, kind=BF16),
            buffer(3, HALO, channels, kind=BF16),
            buffer(3, HALO, channels, kind=BF16),
            buffer(HALO, channels, kind=BF16),
            buffer(TILES, 3, TAPS * 8, 128),
            buffer(4, POLES * 8, 128),
            buffer(2, POLES, TILES * 8, 128),
            buffer(GROUPS, 2, POLES, 8, 128),
            buffer(GROUPS, CHIPS, 2, 8, 128),
            buffer(GROUPS, CHIPS, 2, 8, 128),
            buffer(GROUPS, CHIPS, 2, 8, 128),
            buffer(GROUPS, CHIPS, 2, 8, 128),
            buffer(GROUPS, 2, POLES, 8, 128),
            buffer(GROUPS, 2, POLES, 8, 128),
            buffer(2, POLES, TILES * 8, 128),
            buffer(TILES, GRADS * 8, 128),
            buffer(SUMS, TILES // SUMS // 2, GRADS * 8, 128),
            buffer(SUMS, CHIPS, PIECE, 128),
            buffer(SUMS, CHIPS, PIECE, 128),
            buffer(SUMS, PIECE, 128),
            buffer(SUMS, PIECE, 128),
            buffer(SUMS, LINES, PIECE, 128),
            buffer(SUMS, CHIPS, PIECE, 128),
            buffer(SUMS, CHIPS, PIECE, 128),
            dma(2, 2),
            dma(2, 2),
            dma(3),
            dma(3),
        ]
        + [dma(GROUPS)] * 8
        + [dma(SUMS, 2)] * 2
        + [dma(SUMS)] * 4
        + [dma(SUMS, LINES)] * 2,
        compiler_params=pltpu.CompilerParams(
            collective_id=0, has_side_effects=True, vmem_limit_bytes=60 << 20
        ),
    )(proj, cot, filt, skip, rates, weights)


def local(projected, short_filter, residues, decay_rates, skip_gain, cotangent):
    proj = jnp.transpose(projected[0], (1, 0, 2))
    skip = skip_gain.reshape(TILES * 8, 128)
    output, grad_proj, grad_short, grad_skip = whole(
        proj, cotangent[0], short_filter, skip, decay_rates.T, residues.T
    )
    return (
        output[None],
        jnp.transpose(grad_proj, (1, 0, 2))[None],
        grad_short,
        grad_skip.reshape(skip_gain.shape),
    )


def solution(mesh):
    placed = (P("dp", "ctx", None, None), P(), P(), P(), P(), P("dp", "ctx", None))
    return jax.shard_map(
        local,
        mesh=mesh,
        in_specs=placed,
        out_specs=(P("dp", "ctx", None), P("dp", "ctx", None, None), P(), P()),
        check_vma=False,
    )
```

```python
import jax
import jax.numpy as jnp
from jax import lax
from jax.experimental import pallas as pl
from jax.experimental.pallas import tpu as pltpu
from jax.sharding import PartitionSpec as P

MESH = pl.DeviceIdType.MESH
F32 = jnp.float32
BF16 = jnp.bfloat16
ROWS = 128
HALO = 8
EXT = ROWS + HALO
TILES = 8
WIDE = 1024
POLES = 16
TAPS = 7
CHIPS = 16
LINES = 4
GRADS = 24
GROUPS = 4
SUMS = 2
EARLY = 2
PIECE = TILES // SUMS // 2 * GRADS * 8 // CHIPS


def spread(value, target, row):
    count = value.shape[0]
    for lane in range(8):
        target[pl.ds(row * 8 + lane, count, stride=8), :] = value[:, lane * 128 : (lane + 1) * 128]


def tiles(ref, row, count):
    return ref[pl.ds(pl.multiple_of(row * 8, 8), count * 8), :].reshape(count, 8, 128)


def put_tiles(ref, row, value):
    ref[pl.ds(pl.multiple_of(row * 8, 8), value.shape[0] * 8), :] = value.reshape(-1, 128)


def total(value):
    while value.shape[0] > 1:
        half = value.shape[0] // 2
        value = value[:half] + value[half:]
    return value[0]


def kernel(
    proj, cot, filt, skip, rates, weights,
    outs, gr,
    x, mix, c, yf, yb, ins, fins, prev, nextp, nextc, taps, tables, powers,
    st, st_pair, st_ends, st_came, st_back, st_enter, st_give, st_land,
    gr_pair, gr_cut, gr_came, gr_part, gr_whole, gr_lines, gr_around, gr_land,
    in_sem, halo_send, halo_recv,
    st_ps, st_pr, st_s1, st_r1, st_s2, st_r2, st_ls, st_lr,
    gr_ps, gr_pr, gr_s1, gr_r1, gr_s2, gr_r2, gr_ls, gr_lr,
):
    dp, me = lax.axis_index("dp"), lax.axis_index("ctx")
    count = 2 * CHIPS
    chip, core = lax.div(me, 2), lax.rem(me, 2)
    low = core == 0
    up, down = lax.rem(me + 1, count), lax.rem(me + count - 1, count)
    has_prev = (me > 0).astype(F32)
    has_next = (me < count - 1).astype(F32)

    def remote(source, target, send_sem, recv_sem, line, ctx):
        return pltpu.make_async_remote_copy(
            src_ref=source,
            dst_ref=target,
            send_sem=send_sem,
            recv_sem=recv_sem,
            device_id=(line, ctx),
            device_id_type=MESH,
        )

    barrier = pltpu.get_barrier_semaphore()

    def greet(offset, _):
        other = lax.rem(chip + offset, CHIPS) * 2 + core
        pl.semaphore_signal(barrier, inc=1, device_id=(dp, other), device_id_type=MESH)
        return 0

    lax.fori_loop(1, CHIPS, greet, 0)
    for other in (chip * 2 + 1 - core, up, down):
        pl.semaphore_signal(barrier, inc=1, device_id=(dp, other), device_id_type=MESH)
    for offset in range(1, LINES):
        line = lax.rem(dp + offset, LINES)
        pl.semaphore_signal(barrier, inc=1, device_id=(line, me), device_id_type=MESH)

    def fetch(tile):
        slot = lax.rem(tile, 2)
        lanes = pl.ds(pl.multiple_of(tile * WIDE, WIDE), WIDE)
        return (
            pltpu.make_async_copy(proj.at[:, :, lanes], ins.at[slot, pl.ds(0, 3)], in_sem.at[slot, 0]),
            pltpu.make_async_copy(cot.at[:, lanes], ins.at[slot, 3], in_sem.at[slot, 1]),
            pltpu.make_async_copy(filt.at[:, :, lanes], fins.at[slot], in_sem.at[slot, 2]),
        )

    for tile in range(2):
        for copy in fetch(tile):
            copy.start()

    for quarter in range(4):
        lanes = slice(quarter * 128, (quarter + 1) * 128)
        rate = rates[:, lanes]
        rows = (jnp.exp(-rate), weights[:, lanes], jnp.exp(-rate * ROWS), jnp.exp(-rate * (2 * ROWS)))
        for k in range(4):
            for again in (0, 4):
                tables[k, pl.ds(quarter + again, POLES, stride=8), :] = rows[k]

    def table(k):
        return tables[k].reshape(POLES, 8, 128)

    power = table(0)
    for k in range(8):
        powers[k] = power
        power = power * table(0)

    def short_filter(tile, t, count):
        parts = []
        for j in range(3):
            window = tiles(x.at[tile, j], t + 2, count + 6)
            weight = tiles(taps.at[tile, j], 0, TAPS)
            part = weight[0][None] * window[6 : 6 + count]
            for i in range(1, TAPS):
                part = part + weight[i][None] * window[6 - i : 6 - i + count]
            put_tiles(mix.at[tile, j], t, part)
            parts.append(part)
        return total(tiles(c.at[tile], t, count) * parts[0] * (parts[1] * parts[2]))

    def load_tile(tile):
        slot = lax.rem(tile, 2)
        for copy in fetch(tile):
            copy.wait()
        for j in range(3):
            spread(fins[slot, j], taps.at[tile, j], 0)

        def take(block):
            begin = pl.multiple_of(block * 16, 16)
            for j in range(3):
                spread(ins[slot, j, pl.ds(begin, 16), :].astype(F32), x.at[tile, j], HALO + begin)
            spread(ins[slot, 3, pl.ds(begin, 16), :].astype(F32), c.at[tile], begin)

        def inner(block, acc):
            acc = acc + short_filter(tile, block * 16 - 24, 16)
            take(block)
            return acc

        take(0)
        take(1)
        acc = lax.fori_loop(2, ROWS // 16, inner, jnp.zeros((8, 128), F32))

        @pl.when(tile < TILES - 2)
        def _():
            for copy in fetch(tile + 2):
                copy.start()

        acc = acc + short_filter(tile, ROWS - 24, 16)
        acc = acc + short_filter(tile, ROWS - 8, 8)
        gr[tile, pl.ds(21 * 8, 8), :] = acc
        gr[tile, pl.ds(22 * 8, (GRADS - 22) * 8), :] = jnp.zeros(((GRADS - 22) * 8, 128), F32)

    def load_loop(tile, _):
        load_tile(tile)
        return 0

    lax.fori_loop(0, EARLY, load_loop, 0)
    pl.semaphore_wait(barrier, CHIPS - 1 + 3 + LINES - 1)
    last, first = pl.ds(ROWS - HALO, HALO), pl.ds(0, HALO)
    halo = (
        remote(proj.at[:, last, :], prev, halo_send.at[0], halo_recv.at[0], dp, up),
        remote(proj.at[:, first, :], nextp, halo_send.at[1], halo_recv.at[1], dp, down),
        remote(cot.at[first, :], nextc, halo_send.at[2], halo_recv.at[2], dp, down),
    )
    for copy in halo:
        copy.start()
    lax.fori_loop(EARLY, TILES, load_loop, 0)
    for copy in halo:
        copy.wait()

    def plane_send(source, target, send_sem, recv_sem):
        def start(offset, _):
            other = lax.rem(chip + offset, CHIPS)
            remote(source(other), target.at[chip], send_sem, recv_sem, dp, other * 2 + core).start()
            return 0

        lax.fori_loop(1, CHIPS, start, 0)
        target[chip] = source(chip)[...]

    def plane_wait(target, send_sem, recv_sem):
        most = target.at[pl.ds(0, CHIPS - 1)]
        copy = remote(most, most, send_sem, recv_sem, dp, me)
        copy.wait_recv()
        copy.wait_send()

    pair = chip * 2 + 1 - core

    def mine(group):
        return pl.ds(pl.multiple_of((group * 2 + core) * 8, 8), 8)

    def theirs(group):
        return pl.ds(pl.multiple_of((group * 2 + 1 - core) * 8, 8), 8)

    def st_pair_copy(g):
        return remote(st.at[:, :, theirs(g), :], st_pair.at[g], st_ps.at[g], st_pr.at[g], dp, pair)

    def st_back_copy(g):
        return remote(st_give.at[g], st_land.at[g], st_ls.at[g], st_lr.at[g], dp, pair)

    def low_high(g):
        own, other = st[:, :, mine(g), :], st_pair[g]
        return jnp.where(low, own, other), jnp.where(low, other, own)

    def st_1(g):
        st_pair_copy(g).start()

    def st_2(g):
        st_pair_copy(g).wait()
        lo, hi = low_high(g)
        d = table(2)
        st_ends[g, :, 0] = d * lo[0] + hi[0]
        st_ends[g, :, 1] = lo[1] + d * hi[1]
        plane_send(lambda q: st_ends.at[g, q], st_came.at[g], st_s1.at[g], st_r1.at[g])

    def st_3(g):
        plane_wait(st_came.at[g], st_s1.at[g], st_r1.at[g])
        d2 = tables[3, pl.ds(pl.multiple_of(chip * 8, 8), 8), :]
        s = jnp.zeros((8, 128), F32)
        for q in range(CHIPS):
            st_back[g, q, 0] = s
            s = d2 * s + st_came[g, q, 0]
        s = jnp.zeros((8, 128), F32)
        for q in reversed(range(CHIPS)):
            st_back[g, q, 1] = s
            s = d2 * s + st_came[g, q, 1]
        plane_send(lambda q: st_back.at[g, q], st_enter.at[g], st_s2.at[g], st_r2.at[g])

    def st_4(g):
        plane_wait(st_enter.at[g], st_s2.at[g], st_r2.at[g])
        lo, hi = low_high(g)
        d = table(2)
        fwd, bwd = st_enter[g, :, 0], st_enter[g, :, 1]
        fwd_hi, bwd_lo = d * fwd + lo[0], d * bwd + hi[1]
        st[0, :, mine(g), :] = jnp.where(low, fwd, fwd_hi)
        st[1, :, mine(g), :] = jnp.where(low, bwd_lo, bwd)
        st_give[g, 0] = jnp.where(low, fwd_hi, fwd)
        st_give[g, 1] = jnp.where(low, bwd, bwd_lo)
        st_back_copy(g).start()

    def st_5(g):
        st_back_copy(g).wait()
        st[:, :, theirs(g), :] = st_land[g]

    def st_hooks(slot):
        step = lax.div(slot, 2)
        even = lax.rem(slot, 2) == 0

        @pl.when(jnp.logical_and(even, jnp.logical_and(step >= 3, step < GROUPS + 3)))
        def _():
            st_4(step - 3)

        @pl.when(jnp.logical_and(even, jnp.logical_and(step >= 2, step < GROUPS + 2)))
        def _():
            st_3(step - 2)

        @pl.when(jnp.logical_and(even, jnp.logical_and(step >= 1, step < GROUPS + 1)))
        def _():
            st_2(step - 1)

    def local_scan(tile):
        q, k, v = mix.at[tile, 0], mix.at[tile, 1], mix.at[tile, 2]
        rows = pl.ds(pl.multiple_of(tile * 8, 8), 8)
        gain = skip[rows, :][None]

        def step(block, carry):
            s, b = carry
            begin, end = block * 4, EXT - 4 - block * 4
            a, r = table(0), table(1)
            g = tiles(k, begin, 4) * tiles(v, begin, 4)
            gf = tiles(c.at[tile], end, 4) * tiles(q, end, 4)
            fwd, bwd = [], []
            for u in range(4):
                s = a * s + g[u][None]
                b = a * b + gf[3 - u][None]
                fwd.append(total(r * s))
                bwd.append(total(r * b))
            put_tiles(yf.at[tile], begin, jnp.stack(fwd) + gain * g)
            put_tiles(yb.at[tile], end, jnp.stack(bwd[::-1]) + gain * gf)
            return s, b

        zero = jnp.zeros((POLES, 8, 128), F32)
        s, b = lax.fori_loop(0, ROWS // 4, step, (zero, zero))
        st[0, :, rows, :] = s
        st[1, :, rows, :] = b
        lax.fori_loop(ROWS // 4, EXT // 4, step, (s, b))

    def scan_loop(tile, _):
        lanes = pl.ds(pl.multiple_of(tile * WIDE, WIDE), WIDE)
        for j in range(3):
            spread(prev[j, :, lanes].astype(F32) * has_prev, x.at[tile, j], 0)
            spread(nextp[j, :, lanes].astype(F32) * has_next, x.at[tile, j], HALO + ROWS)
        spread(nextc[:, lanes].astype(F32) * has_next, c.at[tile], ROWS)

        gr[tile, pl.ds(21 * 8, 8), :] += short_filter(tile, 0, 8)
        short_filter(tile, ROWS, 8)
        local_scan(tile)

        @pl.when(lax.rem(tile, 2) == 1)
        def _():
            st_1(lax.div(tile, 2))

        st_hooks(tile)
        return 0

    lax.fori_loop(0, TILES, scan_loop, 0)

    half = TILES // SUMS // 2

    def own(h):
        return pl.ds(h * 2 * half + core * half, half)

    def others(h):
        return pl.ds(h * 2 * half + (1 - core) * half, half)

    def gr_pair_copy(h):
        return remote(gr.at[others(h)], gr_pair.at[h], gr_ps.at[h, 0], gr_pr.at[h, 0], dp, pair)

    def gr_back_copy(h):
        return remote(gr_around.at[h], gr_land.at[h], gr_ps.at[h, 1], gr_pr.at[h, 1], dp, pair)

    def gr_1(h):
        gr_pair_copy(h).start()

    def gr_2(h):
        gr_pair_copy(h).wait()
        gr_cut[h] = (gr[own(h)] + gr_pair[h]).reshape(CHIPS, PIECE, 128)
        plane_send(lambda q: gr_cut.at[h, q], gr_came.at[h], gr_s1.at[h], gr_r1.at[h])

    def line_copy(h, other, slot):
        return remote(gr_part.at[h], gr_lines.at[h, slot], gr_ls.at[h, other], gr_lr.at[h, slot], other, me)

    def gr_3(h):
        plane_wait(gr_came.at[h], gr_s1.at[h], gr_r1.at[h])
        part = gr_came[h, 0]
        for q in range(1, CHIPS):
            part = part + gr_came[h, q]
        gr_part[h] = part
        gr_lines[h, dp] = part
        for offset in range(1, LINES):
            line_copy(h, lax.rem(dp + offset, LINES), dp).start()

    def gr_4(h):
        for offset in range(1, LINES):
            other = lax.rem(dp + offset, LINES)
            line_copy(h, other, other).wait_recv()
            line_copy(h, other, dp).wait_send()
        part = gr_lines[h, 0]
        for q in range(1, LINES):
            part = part + gr_lines[h, q]
        gr_whole[h] = part
        plane_send(lambda q: gr_whole.at[h], gr_around.at[h], gr_s2.at[h], gr_r2.at[h])

    def gr_5(h):
        plane_wait(gr_around.at[h], gr_s2.at[h], gr_r2.at[h])
        gr_back_copy(h).start()

    def gr_6(h):
        gr_back_copy(h).wait()
        gr[own(h)] = gr_around[h].reshape(half, GRADS * 8, 128)
        gr[others(h)] = gr_land[h].reshape(half, GRADS * 8, 128)

    def correct(tile):
        q, k_ref, v = mix.at[tile, 0], mix.at[tile, 1], mix.at[tile, 2]
        rows = pl.ds(pl.multiple_of(tile * 8, 8), 8)

        def step(block, carry):
            e, b = carry
            begin, end = block * 8, EXT - 8 - block * 8
            ahead, behind = [], []
            for k in range(8):
                fwd, bwd = 0, 0
                for n in range(0, POLES, 4):
                    weight = powers[k, n : n + 4]
                    fwd = fwd + weight * e[n : n + 4]
                    bwd = bwd + weight * b[n : n + 4]
                ahead.append(total(fwd))
                behind.append(total(bwd))
            filtered = tiles(yf.at[tile], begin, 8) + jnp.stack(ahead)
            grad_gated = tiles(yb.at[tile], end, 8) + jnp.stack(behind[::-1])
            query, upstream = tiles(q, begin, 8), tiles(c.at[tile], begin, 8)
            key, value = tiles(k_ref, end, 8), tiles(v, end, 8)
            put_tiles(yf.at[tile], begin, query * filtered)
            put_tiles(c.at[tile], begin, upstream * filtered)
            put_tiles(k_ref, end, grad_gated * value)
            put_tiles(v, end, grad_gated * key)
            return powers[7] * e, powers[7] * b

        r = table(1)
        lax.fori_loop(0, EXT // 8, step, (r * st[0, :, rows, :], r * st[1, :, rows, :]))

    def mixed_grad(tile, j):
        return c.at[tile] if j == 0 else mix.at[tile, j]

    def tap_grads(tile):
        for j in range(3):

            def body(block, acc):
                t = block * 16
                grad = tiles(mixed_grad(tile, j), t, 16)
                window = tiles(x.at[tile, j], t + 2, 22)
                return tuple(acc[i] + total(grad * window[6 - i : 22 - i]) for i in range(TAPS))

            acc = lax.fori_loop(0, ROWS // 16, body, (jnp.zeros((8, 128), F32),) * TAPS)
            for i in range(TAPS):
                gr[tile, pl.ds((j * TAPS + i) * 8, 8), :] = acc[i]

    stages = (gr_1, gr_2, gr_3, gr_4, gr_5, gr_6)
    plan = {
        3: ((1, 0),),
        4: ((2, 0),),
        6: ((3, 0),),
        7: ((1, 1), (4, 0)),
        8: ((2, 1),),
        11: ((5, 0),),
        12: ((3, 1),),
        13: ((6, 0),),
        15: ((4, 1),),
    }

    def gr_hooks(tile, offset):
        for slot, todo in plan.items():
            if offset <= slot < offset + TILES:

                @pl.when(tile == slot - offset)
                def _(todo=todo):
                    for stage, h in todo:
                        stages[stage - 1](h)

    def post_loop(tile, _):
        @pl.when(lax.rem(tile, 2) == 0)
        def _():
            st_5(lax.div(tile, 2))

        correct(tile)
        tap_grads(tile)
        st_hooks(tile + TILES)
        gr_hooks(tile, 0)
        return 0

    lax.fori_loop(0, TILES, post_loop, 0)

    def out_loop(tile, _):
        def filter_rows(j, block):
            t = block * 16
            ahead = tiles(mixed_grad(tile, j), t, 22)
            weight = tiles(taps.at[tile, j], 0, TAPS)
            part = weight[0][None] * ahead[0:16]
            for i in range(1, TAPS):
                part = part + weight[i][None] * ahead[i : i + 16]
            put_tiles(x.at[tile, j], t, part)

        def give(source, j, block):
            begin = pl.multiple_of(block * 16, 16)
            for lane in range(8):
                value = source[pl.ds(begin * 8 + lane, 16, stride=8), :]
                lanes = pl.ds(pl.multiple_of(tile * WIDE + lane * 128, 128), 128)
                outs[j, pl.ds(begin, 16), lanes] = value.astype(BF16)

        def body(block, _):
            for j in range(3):
                give(x.at[tile, j], j, block - 1)
            give(yf.at[tile], 3, block)
            for j in range(3):
                filter_rows(j, block)
            return 0

        for j in range(3):
            filter_rows(j, 0)
        give(yf.at[tile], 3, 0)
        lax.fori_loop(1, ROWS // 16, body, 0)
        for j in range(3):
            give(x.at[tile, j], j, ROWS // 16 - 1)

        gr_hooks(tile, TILES)
        return 0

    lax.fori_loop(0, TILES, out_loop, 0)
    gr_5(1)
    gr_6(1)


def leave_kernel(outs, gr, output, grad_proj, grad_short, grad_skip, sem):
    copies = [
        pltpu.make_async_copy(outs.at[j], grad_proj.at[j], sem.at[j]) for j in range(3)
    ] + [pltpu.make_async_copy(outs.at[3], output, sem.at[3])]
    for copy in copies:
        copy.start()
    for tile in range(TILES):
        grad_skip[tile * 8 : tile * 8 + 8, :] = gr[tile, 21 * 8 : 22 * 8, :]
        for j in range(3):
            for lane in range(8):
                value = gr[tile, pl.ds(j * TAPS * 8 + lane, TAPS, stride=8), :]
                begin = tile * WIDE + lane * 128
                grad_short[j, :, begin : begin + 128] = value
    for copy in copies:
        copy.wait()


def leave(outs, gr):
    channels = outs.shape[2]
    anywhere = pl.BlockSpec(memory_space=pl.ANY)
    vmem = pl.BlockSpec(memory_space=pltpu.VMEM)
    return pl.pallas_call(
        leave_kernel,
        name="leave",
        out_shape=(
            jax.ShapeDtypeStruct((ROWS, channels), BF16),
            jax.ShapeDtypeStruct((3, ROWS, channels), BF16),
            jax.ShapeDtypeStruct((3, TAPS, channels), F32),
            jax.ShapeDtypeStruct((TILES * 8, 128), F32),
        ),
        in_specs=[vmem, vmem],
        out_specs=(anywhere, anywhere, vmem, vmem),
        scratch_shapes=[pltpu.SemaphoreType.DMA((4,))],
        compiler_params=pltpu.CompilerParams(vmem_limit_bytes=4 << 20),
    )(
        pltpu.with_memory_space_constraint(outs, pltpu.VMEM),
        pltpu.with_memory_space_constraint(gr, pltpu.VMEM),
    )


def whole(proj, cot, filt, skip, rates, weights):
    channels = proj.shape[2]
    anywhere = pl.BlockSpec(memory_space=pl.ANY)
    vmem = pl.BlockSpec(memory_space=pltpu.VMEM)

    def buffer(*shape, kind=F32):
        return pltpu.VMEM(shape, kind)

    def dma(*shape):
        return pltpu.SemaphoreType.DMA(shape)

    return pl.pallas_call(
        kernel,
        name="hyena",
        out_shape=(
            buffer(4, ROWS, channels, kind=BF16),
            buffer(TILES, GRADS * 8, 128),
        ),
        in_specs=[anywhere, anywhere, anywhere, vmem, vmem, vmem],
        out_specs=(vmem, vmem),
        scratch_shapes=[
            buffer(TILES, 3, (EXT + HALO) * 8, 128),
            buffer(TILES, 3, EXT * 8, 128),
            buffer(TILES, EXT * 8, 128),
            buffer(TILES, EXT * 8, 128),
            buffer(TILES, EXT * 8, 128),
            buffer(2, 4, ROWS, WIDE, kind=BF16),
            buffer(2, 3, TAPS, WIDE),
            buffer(3, HALO, channels, kind=BF16),
            buffer(3, HALO, channels, kind=BF16),
            buffer(HALO, channels, kind=BF16),
            buffer(TILES, 3, TAPS * 8, 128),
            buffer(4, POLES * 8, 128),
            buffer(8, POLES, 8, 128),
            buffer(2, POLES, TILES * 8, 128),
            buffer(GROUPS, 2, POLES, 8, 128),
            buffer(GROUPS, CHIPS, 2, 8, 128),
            buffer(GROUPS, CHIPS, 2, 8, 128),
            buffer(GROUPS, CHIPS, 2, 8, 128),
            buffer(GROUPS, CHIPS, 2, 8, 128),
            buffer(GROUPS, 2, POLES, 8, 128),
            buffer(GROUPS, 2, POLES, 8, 128),
            buffer(SUMS, TILES // SUMS // 2, GRADS * 8, 128),
            buffer(SUMS, CHIPS, PIECE, 128),
            buffer(SUMS, CHIPS, PIECE, 128),
            buffer(SUMS, PIECE, 128),
            buffer(SUMS, PIECE, 128),
            buffer(SUMS, LINES, PIECE, 128),
            buffer(SUMS, CHIPS, PIECE, 128),
            buffer(SUMS, CHIPS, PIECE, 128),
            dma(2, 3),
            dma(3),
            dma(3),
        ]
        + [dma(GROUPS)] * 8
        + [dma(SUMS, 2)] * 2
        + [dma(SUMS)] * 4
        + [dma(SUMS, LINES)] * 2,
        compiler_params=pltpu.CompilerParams(
            collective_id=0, has_side_effects=True, vmem_limit_bytes=52 << 20
        ),
    )(proj, cot, filt, skip, rates, weights)


def local(projected, short_filter, residues, decay_rates, skip_gain, cotangent):
    proj = jnp.transpose(projected[0], (1, 0, 2))
    skip = skip_gain.reshape(TILES * 8, 128)
    outs, grads = whole(proj, cotangent[0], short_filter, skip, decay_rates.T, residues.T)
    output, grad_proj, grad_short, grad_skip = leave(outs, grads)
    return (
        output[None],
        jnp.transpose(grad_proj, (1, 0, 2))[None],
        grad_short,
        grad_skip.reshape(skip_gain.shape),
    )


def solution(mesh):
    placed = (P("dp", "ctx", None, None), P(), P(), P(), P(), P("dp", "ctx", None))
    return jax.shard_map(
        local,
        mesh=mesh,
        in_specs=placed,
        out_specs=(P("dp", "ctx", None), P("dp", "ctx", None, None), P(), P()),
        check_vma=False,
    )
```

```python
import jax
import jax.numpy as jnp
from jax import lax
from jax.experimental import pallas as pl
from jax.experimental.pallas import tpu as pltpu
from jax.sharding import PartitionSpec as P

MESH = pl.DeviceIdType.MESH
F32 = jnp.float32
BF16 = jnp.bfloat16
ROWS = 128
HALO = 8
EXT = ROWS + HALO
TILES = 8
WIDE = 1024
POLES = 16
TAPS = 7
CHIPS = 16
LINES = 4
GRADS = 32
GROUPS = 4
SUMS = ((0, 4, 24), (4, 2, 32), (6, 2, 32))
FAR = (10, 6, 14, 9, 11, 2, 8, 5, 7, 13, 15, 1, 3, 4, 12)
EARLY = 2
PIECES = tuple(many // 2 * rows * 8 // CHIPS for _, many, rows in SUMS)


def spread(value, target, row):
    count = value.shape[0]
    for lane in range(8):
        target[pl.ds(row * 8 + lane, count, stride=8), :] = value[:, lane * 128 : (lane + 1) * 128]


def tiles(ref, row, count):
    return ref[pl.ds(pl.multiple_of(row * 8, 8), count * 8), :].reshape(count, 8, 128)


def put_tiles(ref, row, value):
    ref[pl.ds(pl.multiple_of(row * 8, 8), value.shape[0] * 8), :] = value.reshape(-1, 128)


def total(value):
    while value.shape[0] > 1:
        half = value.shape[0] // 2
        value = value[:half] + value[half:]
    return value[0]


def kernel(
    proj, cot, filt, skip, rates, weights,
    outs, gr,
    x, mix, c, yf, yb, ins, fins, prev, nextp, nextc, taps, tables, powers,
    st, st_pair, st_ends, st_came, st_back, st_enter, st_give, st_land,
    gr_pair, gr_cut, gr_came, gr_part, gr_whole, gr_lines, gr_around, gr_land,
    in_sem, halo_send, halo_recv,
    st_ps, st_pr, st_s1, st_r1, st_s2, st_r2, st_ls, st_lr,
    gr_ps, gr_pr, gr_s1, gr_r1, gr_s2, gr_r2, gr_ls, gr_lr,
):
    dp, me = lax.axis_index("dp"), lax.axis_index("ctx")
    count = 2 * CHIPS
    chip, core = lax.div(me, 2), lax.rem(me, 2)
    low = core == 0
    up, down = lax.rem(me + 1, count), lax.rem(me + count - 1, count)
    has_prev = (me > 0).astype(F32)
    has_next = (me < count - 1).astype(F32)

    def remote(source, target, send_sem, recv_sem, line, ctx):
        return pltpu.make_async_remote_copy(
            src_ref=source,
            dst_ref=target,
            send_sem=send_sem,
            recv_sem=recv_sem,
            device_id=(line, ctx),
            device_id_type=MESH,
        )

    barrier = pltpu.get_barrier_semaphore()

    def greet(offset, _):
        other = lax.rem(chip + offset, CHIPS) * 2 + core
        pl.semaphore_signal(barrier, inc=1, device_id=(dp, other), device_id_type=MESH)
        return 0

    lax.fori_loop(1, CHIPS, greet, 0)
    for other in (chip * 2 + 1 - core, up, down):
        pl.semaphore_signal(barrier, inc=1, device_id=(dp, other), device_id_type=MESH)
    for offset in range(1, LINES):
        line = lax.rem(dp + offset, LINES)
        pl.semaphore_signal(barrier, inc=1, device_id=(line, me), device_id_type=MESH)

    def fetch(tile):
        slot = lax.rem(tile, 2)
        lanes = pl.ds(pl.multiple_of(tile * WIDE, WIDE), WIDE)
        return (
            pltpu.make_async_copy(proj.at[:, :, lanes], ins.at[slot, pl.ds(0, 3)], in_sem.at[slot, 0]),
            pltpu.make_async_copy(cot.at[:, lanes], ins.at[slot, 3], in_sem.at[slot, 1]),
            pltpu.make_async_copy(filt.at[:, :, lanes], fins.at[slot], in_sem.at[slot, 2]),
        )

    for tile in range(2):
        for copy in fetch(tile):
            copy.start()

    for quarter in range(4):
        lanes = slice(quarter * 128, (quarter + 1) * 128)
        rate = rates[:, lanes]
        rows = (jnp.exp(-rate), weights[:, lanes], jnp.exp(-rate * ROWS), jnp.exp(-rate * (2 * ROWS)))
        for k in range(4):
            for again in (0, 4):
                tables[k, pl.ds(quarter + again, POLES, stride=8), :] = rows[k]

    def table(k):
        return tables[k].reshape(POLES, 8, 128)

    power = table(0)
    for k in range(8):
        powers[k] = power
        power = power * table(0)

    def short_filter(tile, t, count):
        parts = []
        for j in range(3):
            window = tiles(x.at[tile, j], t + 2, count + 6)
            weight = tiles(taps.at[tile, j], 0, TAPS)
            part = weight[0][None] * window[6 : 6 + count]
            for i in range(1, TAPS):
                part = part + weight[i][None] * window[6 - i : 6 - i + count]
            put_tiles(mix.at[tile, j], t, part)
            parts.append(part)
        return total(tiles(c.at[tile], t, count) * parts[0] * (parts[1] * parts[2]))

    def load_tile(tile):
        slot = lax.rem(tile, 2)
        for copy in fetch(tile):
            copy.wait()
        for j in range(3):
            spread(fins[slot, j], taps.at[tile, j], 0)

        def take(block):
            begin = pl.multiple_of(block * 16, 16)
            for j in range(3):
                spread(ins[slot, j, pl.ds(begin, 16), :].astype(F32), x.at[tile, j], HALO + begin)
            spread(ins[slot, 3, pl.ds(begin, 16), :].astype(F32), c.at[tile], begin)

        def inner(block, acc):
            acc = acc + short_filter(tile, block * 16 - 24, 16)
            take(block)
            return acc

        take(0)
        take(1)
        acc = lax.fori_loop(2, ROWS // 16, inner, jnp.zeros((8, 128), F32))

        @pl.when(tile < TILES - 2)
        def _():
            for copy in fetch(tile + 2):
                copy.start()

        acc = acc + short_filter(tile, ROWS - 24, 16)
        acc = acc + short_filter(tile, ROWS - 8, 8)
        gr[tile, pl.ds(21 * 8, 8), :] = acc
        gr[tile, pl.ds(22 * 8, (GRADS - 22) * 8), :] = jnp.zeros(((GRADS - 22) * 8, 128), F32)

    def load_loop(tile, _):
        load_tile(tile)
        return 0

    lax.fori_loop(0, EARLY, load_loop, 0)
    pl.semaphore_wait(barrier, CHIPS - 1 + 3 + LINES - 1)
    last, first = pl.ds(ROWS - HALO, HALO), pl.ds(0, HALO)
    halo = (
        remote(proj.at[:, last, :], prev, halo_send.at[0], halo_recv.at[0], dp, up),
        remote(proj.at[:, first, :], nextp, halo_send.at[1], halo_recv.at[1], dp, down),
        remote(cot.at[first, :], nextc, halo_send.at[2], halo_recv.at[2], dp, down),
    )
    for copy in halo:
        copy.start()
    lax.fori_loop(EARLY, TILES, load_loop, 0)
    for copy in halo:
        copy.wait()

    def plane_send(source, target, send_sem, recv_sem):
        def start(offset, _):
            other = lax.rem(chip + offset, CHIPS)
            remote(source(other), target.at[chip], send_sem, recv_sem, dp, other * 2 + core).start()
            return 0

        for offset in FAR:
            start(offset, 0)
        target[chip] = source(chip)[...]

    def plane_wait(target, send_sem, recv_sem):
        most = target.at[pl.ds(0, CHIPS - 1)]
        copy = remote(most, most, send_sem, recv_sem, dp, me)
        copy.wait_recv()
        copy.wait_send()

    pair = chip * 2 + 1 - core

    def mine(group):
        return pl.ds(pl.multiple_of((group * 2 + core) * 8, 8), 8)

    def theirs(group):
        return pl.ds(pl.multiple_of((group * 2 + 1 - core) * 8, 8), 8)

    def st_pair_copy(g):
        return remote(st.at[:, :, theirs(g), :], st_pair.at[g], st_ps.at[g], st_pr.at[g], dp, pair)

    def st_back_copy(g):
        return remote(st_give.at[g], st_land.at[g], st_ls.at[g], st_lr.at[g], dp, pair)

    def low_high(g):
        own, other = st[:, :, mine(g), :], st_pair[g]
        return jnp.where(low, own, other), jnp.where(low, other, own)

    def st_1(g):
        st_pair_copy(g).start()

    def st_2(g):
        st_pair_copy(g).wait()
        lo, hi = low_high(g)
        d = table(2)
        st_ends[g, :, 0] = d * lo[0] + hi[0]
        st_ends[g, :, 1] = lo[1] + d * hi[1]
        plane_send(lambda q: st_ends.at[g, q], st_came.at[g], st_s1.at[g], st_r1.at[g])

    def st_3(g):
        plane_wait(st_came.at[g], st_s1.at[g], st_r1.at[g])
        d2 = tables[3, pl.ds(pl.multiple_of(chip * 8, 8), 8), :]
        s = jnp.zeros((8, 128), F32)
        for q in range(CHIPS):
            st_back[g, q, 0] = s
            s = d2 * s + st_came[g, q, 0]
        s = jnp.zeros((8, 128), F32)
        for q in reversed(range(CHIPS)):
            st_back[g, q, 1] = s
            s = d2 * s + st_came[g, q, 1]
        plane_send(lambda q: st_back.at[g, q], st_enter.at[g], st_s2.at[g], st_r2.at[g])

    def st_4(g):
        plane_wait(st_enter.at[g], st_s2.at[g], st_r2.at[g])
        lo, hi = low_high(g)
        d = table(2)
        fwd, bwd = st_enter[g, :, 0], st_enter[g, :, 1]
        fwd_hi, bwd_lo = d * fwd + lo[0], d * bwd + hi[1]
        st[0, :, mine(g), :] = jnp.where(low, fwd, fwd_hi)
        st[1, :, mine(g), :] = jnp.where(low, bwd_lo, bwd)
        st_give[g, 0] = jnp.where(low, fwd_hi, fwd)
        st_give[g, 1] = jnp.where(low, bwd, bwd_lo)
        st_back_copy(g).start()

    def st_5(g):
        st_back_copy(g).wait()
        st[:, :, theirs(g), :] = st_land[g]

    def st_hooks(slot):
        step = lax.div(slot, 2)
        even = lax.rem(slot, 2) == 0

        @pl.when(jnp.logical_and(even, jnp.logical_and(step >= 1, step < GROUPS + 1)))
        def _():
            st_2(step - 1)

        @pl.when(jnp.logical_and(even, jnp.logical_and(step >= 2, step < GROUPS + 2)))
        def _():
            st_3(step - 2)

        @pl.when(jnp.logical_and(even, jnp.logical_and(step >= 3, step < GROUPS + 3)))
        def _():
            st_4(step - 3)

    def local_scan(tile):
        q, k, v = mix.at[tile, 0], mix.at[tile, 1], mix.at[tile, 2]
        rows = pl.ds(pl.multiple_of(tile * 8, 8), 8)
        gain = skip[rows, :][None]

        def step(block, carry):
            s, b = carry
            begin, end = block * 4, EXT - 4 - block * 4
            a, r = table(0), table(1)
            g = tiles(k, begin, 4) * tiles(v, begin, 4)
            gf = tiles(c.at[tile], end, 4) * tiles(q, end, 4)
            fwd, bwd = [], []
            for u in range(4):
                s = a * s + g[u][None]
                b = a * b + gf[3 - u][None]
                fwd.append(total(r * s))
                bwd.append(total(r * b))
            put_tiles(yf.at[tile], begin, jnp.stack(fwd) + gain * g)
            put_tiles(yb.at[tile], end, jnp.stack(bwd[::-1]) + gain * gf)
            return s, b

        zero = jnp.zeros((POLES, 8, 128), F32)
        s, b = lax.fori_loop(0, ROWS // 4, step, (zero, zero))
        st[0, :, rows, :] = s
        st[1, :, rows, :] = b
        lax.fori_loop(ROWS // 4, EXT // 4, step, (s, b))

    def scan_loop(tile, _):
        lanes = pl.ds(pl.multiple_of(tile * WIDE, WIDE), WIDE)
        for j in range(3):
            spread(prev[j, :, lanes].astype(F32) * has_prev, x.at[tile, j], 0)
            spread(nextp[j, :, lanes].astype(F32) * has_next, x.at[tile, j], HALO + ROWS)
        spread(nextc[:, lanes].astype(F32) * has_next, c.at[tile], ROWS)

        gr[tile, pl.ds(21 * 8, 8), :] += short_filter(tile, 0, 8)
        short_filter(tile, ROWS, 8)
        local_scan(tile)

        @pl.when(lax.rem(tile, 2) == 1)
        def _():
            st_1(lax.div(tile, 2))

        st_hooks(tile)
        return 0

    lax.fori_loop(0, TILES, scan_loop, 0)

    def gr_half(h, which):
        begin, many, rows = SUMS[h]
        half = many // 2
        return gr.at[pl.ds(begin + which * half, half), pl.ds(0, rows * 8), :]

    def gr_pair_copy(h):
        return remote(gr_half(h, 1 - core), gr_pair[h], gr_ps.at[h, 0], gr_pr.at[h, 0], dp, pair)

    def gr_back_copy(h):
        return remote(gr_around[h], gr_land[h], gr_ps.at[h, 1], gr_pr.at[h, 1], dp, pair)

    def gr_1(h):
        gr_pair_copy(h).start()

    def gr_2(h):
        gr_pair_copy(h).wait()
        both = gr_half(h, core)[...] + gr_pair[h][...]
        gr_cut[h][...] = both.reshape(CHIPS, PIECES[h], 128)
        plane_send(lambda q: gr_cut[h].at[q], gr_came[h], gr_s1.at[h], gr_r1.at[h])

    def line_copy(h, other, slot):
        return remote(gr_part[h], gr_lines[h].at[slot], gr_ls.at[h, other], gr_lr.at[h, slot], other, me)

    def gr_3(h):
        plane_wait(gr_came[h], gr_s1.at[h], gr_r1.at[h])
        part = gr_came[h][0]
        for q in range(1, CHIPS):
            part = part + gr_came[h][q]
        gr_part[h][...] = part
        gr_lines[h][dp] = part
        for offset in range(1, LINES):
            line_copy(h, lax.rem(dp + offset, LINES), dp).start()

    def gr_4(h):
        for offset in range(1, LINES):
            other = lax.rem(dp + offset, LINES)
            line_copy(h, other, other).wait_recv()
            line_copy(h, other, dp).wait_send()
        part = gr_lines[h][0]
        for q in range(1, LINES):
            part = part + gr_lines[h][q]
        gr_whole[h][...] = part
        plane_send(lambda q: gr_whole[h], gr_around[h], gr_s2.at[h], gr_r2.at[h])

    def gr_5(h):
        plane_wait(gr_around[h], gr_s2.at[h], gr_r2.at[h])
        gr_back_copy(h).start()

    def gr_6(h):
        gr_back_copy(h).wait()
        _, many, rows = SUMS[h]
        gr_half(h, core)[...] = gr_around[h][...].reshape(many // 2, rows * 8, 128)
        gr_half(h, 1 - core)[...] = gr_land[h][...].reshape(many // 2, rows * 8, 128)

    def correct(tile):
        q, k_ref, v = mix.at[tile, 0], mix.at[tile, 1], mix.at[tile, 2]
        rows = pl.ds(pl.multiple_of(tile * 8, 8), 8)

        def step(block, carry):
            e, b = carry
            begin, end = block * 8, EXT - 8 - block * 8
            ahead, behind = [], []
            for k in range(8):
                fwd, bwd = 0, 0
                for n in range(0, POLES, 4):
                    weight = powers[k, n : n + 4]
                    fwd = fwd + weight * e[n : n + 4]
                    bwd = bwd + weight * b[n : n + 4]
                ahead.append(total(fwd))
                behind.append(total(bwd))
            filtered = tiles(yf.at[tile], begin, 8) + jnp.stack(ahead)
            grad_gated = tiles(yb.at[tile], end, 8) + jnp.stack(behind[::-1])
            query, upstream = tiles(q, begin, 8), tiles(c.at[tile], begin, 8)
            key, value = tiles(k_ref, end, 8), tiles(v, end, 8)
            put_tiles(yf.at[tile], begin, query * filtered)
            put_tiles(c.at[tile], begin, upstream * filtered)
            put_tiles(k_ref, end, grad_gated * value)
            put_tiles(v, end, grad_gated * key)
            return powers[7] * e, powers[7] * b

        r = table(1)
        lax.fori_loop(0, EXT // 8, step, (r * st[0, :, rows, :], r * st[1, :, rows, :]))

    def mixed_grad(tile, j):
        return c.at[tile] if j == 0 else mix.at[tile, j]

    def tap_grads(tile):
        for j in range(3):

            def body(block, acc):
                t = block * 16
                grad = tiles(mixed_grad(tile, j), t, 16)
                window = tiles(x.at[tile, j], t + 2, 22)
                return tuple(acc[i] + total(grad * window[6 - i : 22 - i]) for i in range(TAPS))

            acc = lax.fori_loop(0, ROWS // 16, body, (jnp.zeros((8, 128), F32),) * TAPS)
            for i in range(TAPS):
                gr[tile, pl.ds((j * TAPS + i) * 8, 8), :] = acc[i]

    stages = (gr_1, gr_2, gr_3, gr_4, gr_5, gr_6)
    plan = {
        3: ((1, 0),),
        5: ((2, 0), (1, 1)),
        6: ((2, 1),),
        7: ((1, 2), (3, 0)),
        8: ((2, 2), (3, 1)),
        9: ((4, 0),),
        11: ((4, 1),),
        12: ((3, 2),),
        13: ((5, 0),),
        15: ((4, 2), (6, 0), (5, 1)),
    }

    def gr_hooks(tile, offset):
        for slot, todo in plan.items():
            if offset <= slot < offset + TILES:

                @pl.when(tile == slot - offset)
                def _(todo=todo):
                    for stage, h in todo:
                        stages[stage - 1](h)

    def post_loop(tile, _):
        @pl.when(lax.rem(tile, 2) == 0)
        def _():
            st_5(lax.div(tile, 2))

        correct(tile)
        tap_grads(tile)
        st_hooks(tile + TILES)
        gr_hooks(tile, 0)
        return 0

    lax.fori_loop(0, TILES, post_loop, 0)

    def out_loop(tile, _):
        def filter_rows(j, block):
            t = block * 16
            ahead = tiles(mixed_grad(tile, j), t, 22)
            weight = tiles(taps.at[tile, j], 0, TAPS)
            part = weight[0][None] * ahead[0:16]
            for i in range(1, TAPS):
                part = part + weight[i][None] * ahead[i : i + 16]
            put_tiles(x.at[tile, j], t, part)

        def give(source, j, block):
            begin = pl.multiple_of(block * 16, 16)
            for lane in range(8):
                value = source[pl.ds(begin * 8 + lane, 16, stride=8), :]
                lanes = pl.ds(pl.multiple_of(tile * WIDE + lane * 128, 128), 128)
                outs[j, pl.ds(begin, 16), lanes] = value.astype(BF16)

        def body(block, _):
            for j in range(3):
                give(x.at[tile, j], j, block - 1)
            give(yf.at[tile], 3, block)
            for j in range(3):
                filter_rows(j, block)
            return 0

        for j in range(3):
            filter_rows(j, 0)
        give(yf.at[tile], 3, 0)
        lax.fori_loop(1, ROWS // 16, body, 0)
        for j in range(3):
            give(x.at[tile, j], j, ROWS // 16 - 1)

        gr_hooks(tile, TILES)
        return 0

    lax.fori_loop(0, TILES, out_loop, 0)
    gr_6(1)
    gr_5(2)
    gr_6(2)


def leave_kernel(outs, gr, output, grad_proj, grad_short, grad_skip, sem):
    copies = [
        pltpu.make_async_copy(outs.at[j], grad_proj.at[j], sem.at[j]) for j in range(3)
    ] + [pltpu.make_async_copy(outs.at[3], output, sem.at[3])]
    for copy in copies:
        copy.start()
    for tile in range(TILES):
        grad_skip[tile * 8 : tile * 8 + 8, :] = gr[tile, 21 * 8 : 22 * 8, :]
        for j in range(3):
            for lane in range(8):
                value = gr[tile, pl.ds(j * TAPS * 8 + lane, TAPS, stride=8), :]
                begin = tile * WIDE + lane * 128
                grad_short[j, :, begin : begin + 128] = value
    for copy in copies:
        copy.wait()


def leave(outs, gr):
    channels = outs.shape[2]
    anywhere = pl.BlockSpec(memory_space=pl.ANY)
    vmem = pl.BlockSpec(memory_space=pltpu.VMEM)
    return pl.pallas_call(
        leave_kernel,
        name="leave",
        out_shape=(
            jax.ShapeDtypeStruct((ROWS, channels), BF16),
            jax.ShapeDtypeStruct((3, ROWS, channels), BF16),
            jax.ShapeDtypeStruct((3, TAPS, channels), F32),
            jax.ShapeDtypeStruct((TILES * 8, 128), F32),
        ),
        in_specs=[vmem, vmem],
        out_specs=(anywhere, anywhere, vmem, vmem),
        scratch_shapes=[pltpu.SemaphoreType.DMA((4,))],
        compiler_params=pltpu.CompilerParams(vmem_limit_bytes=4 << 20),
    )(
        pltpu.with_memory_space_constraint(outs, pltpu.VMEM),
        pltpu.with_memory_space_constraint(gr, pltpu.VMEM),
    )


def whole(proj, cot, filt, skip, rates, weights):
    channels = proj.shape[2]
    anywhere = pl.BlockSpec(memory_space=pl.ANY)
    vmem = pl.BlockSpec(memory_space=pltpu.VMEM)

    def buffer(*shape, kind=F32):
        return pltpu.VMEM(shape, kind)

    def dma(*shape):
        return pltpu.SemaphoreType.DMA(shape)

    slots = tuple(buffer(CHIPS, piece, 128) for piece in PIECES)
    pieces = tuple(buffer(piece, 128) for piece in PIECES)
    return pl.pallas_call(
        kernel,
        name="hyena",
        out_shape=(
            buffer(4, ROWS, channels, kind=BF16),
            buffer(TILES, GRADS * 8, 128),
        ),
        in_specs=[anywhere, anywhere, anywhere, vmem, vmem, vmem],
        out_specs=(vmem, vmem),
        scratch_shapes=[
            buffer(TILES, 3, (EXT + HALO) * 8, 128),
            buffer(TILES, 3, EXT * 8, 128),
            buffer(TILES, EXT * 8, 128),
            buffer(TILES, EXT * 8, 128),
            buffer(TILES, EXT * 8, 128),
            buffer(2, 4, ROWS, WIDE, kind=BF16),
            buffer(2, 3, TAPS, WIDE),
            buffer(3, HALO, channels, kind=BF16),
            buffer(3, HALO, channels, kind=BF16),
            buffer(HALO, channels, kind=BF16),
            buffer(TILES, 3, TAPS * 8, 128),
            buffer(4, POLES * 8, 128),
            buffer(8, POLES, 8, 128),
            buffer(2, POLES, TILES * 8, 128),
            buffer(GROUPS, 2, POLES, 8, 128),
            buffer(GROUPS, CHIPS, 2, 8, 128),
            buffer(GROUPS, CHIPS, 2, 8, 128),
            buffer(GROUPS, CHIPS, 2, 8, 128),
            buffer(GROUPS, CHIPS, 2, 8, 128),
            buffer(GROUPS, 2, POLES, 8, 128),
            buffer(GROUPS, 2, POLES, 8, 128),
            tuple(buffer(many // 2, rows * 8, 128) for _, many, rows in SUMS),
            slots,
            slots,
            pieces,
            pieces,
            tuple(buffer(LINES, piece, 128) for piece in PIECES),
            slots,
            slots,
            dma(2, 3),
            dma(3),
            dma(3),
        ]
        + [dma(GROUPS)] * 8
        + [dma(len(SUMS), 2)] * 2
        + [dma(len(SUMS))] * 4
        + [dma(len(SUMS), LINES)] * 2,
        compiler_params=pltpu.CompilerParams(
            collective_id=0, has_side_effects=True, vmem_limit_bytes=52 << 20
        ),
    )(proj, cot, filt, skip, rates, weights)


def local(projected, short_filter, residues, decay_rates, skip_gain, cotangent):
    proj = jnp.transpose(projected[0], (1, 0, 2))
    skip = skip_gain.reshape(TILES * 8, 128)
    outs, grads = whole(proj, cotangent[0], short_filter, skip, decay_rates.T, residues.T)
    output, grad_proj, grad_short, grad_skip = leave(outs, grads)
    return (
        output[None],
        jnp.transpose(grad_proj, (1, 0, 2))[None],
        grad_short,
        grad_skip.reshape(skip_gain.shape),
    )


def solution(mesh):
    placed = (P("dp", "ctx", None, None), P(), P(), P(), P(), P("dp", "ctx", None))
    return jax.shard_map(
        local,
        mesh=mesh,
        in_specs=placed,
        out_specs=(P("dp", "ctx", None), P("dp", "ctx", None, None), P(), P()),
        check_vma=False,
    )
```

```python
import jax
import jax.numpy as jnp
from jax import lax
from jax.experimental import pallas as pl
from jax.experimental.pallas import tpu as pltpu
from jax.sharding import PartitionSpec as P

MESH = pl.DeviceIdType.MESH
F32 = jnp.float32
BF16 = jnp.bfloat16
ROWS = 128
HALO = 8
EXT = ROWS + HALO
TILES = 8
WIDE = 1024
POLES = 16
TAPS = 7
CHIPS = 16
LINES = 4
GRADS = 32
GROUPS = 4
SUMS = ((0, 4, 24), (4, 2, 32), (6, 2, 32))
FAR = (10, 6, 14, 9, 11, 2, 8, 5, 7, 13, 15, 1, 3, 4, 12)
EARLY = 2
PIECES = tuple(many // 2 * rows * 8 // CHIPS for _, many, rows in SUMS)


def spread(value, target, row):
    count = value.shape[0]
    for lane in range(8):
        target[pl.ds(row * 8 + lane, count, stride=8), :] = value[:, lane * 128 : (lane + 1) * 128]


def tiles(ref, row, count):
    return ref[pl.ds(pl.multiple_of(row * 8, 8), count * 8), :].reshape(count, 8, 128)


def put_tiles(ref, row, value):
    ref[pl.ds(pl.multiple_of(row * 8, 8), value.shape[0] * 8), :] = value.reshape(-1, 128)


def total(value):
    while value.shape[0] > 1:
        half = value.shape[0] // 2
        value = value[:half] + value[half:]
    return value[0]


def kernel(
    proj, cot, filt, skip, rates, weights,
    outs, gr,
    x, mix, c, yf, yb, ins, fins, prev, nextp, nextc, taps, tables, powers,
    st, st_pair, st_ends, st_came, st_back, st_enter, st_give, st_land,
    gr_pair, gr_cut, gr_came, gr_part, gr_whole, gr_lines, gr_around, gr_land,
    in_sem, halo_send, halo_recv,
    st_ps, st_pr, st_s1, st_r1, st_s2, st_r2, st_ls, st_lr,
    gr_ps, gr_pr, gr_s1, gr_r1, gr_s2, gr_r2, gr_ls, gr_lr,
):
    dp, me = lax.axis_index("dp"), lax.axis_index("ctx")
    count = 2 * CHIPS
    chip, core = lax.div(me, 2), lax.rem(me, 2)
    low = core == 0
    up, down = lax.rem(me + 1, count), lax.rem(me + count - 1, count)
    has_prev = (me > 0).astype(F32)
    has_next = (me < count - 1).astype(F32)

    def remote(source, target, send_sem, recv_sem, line, ctx):
        return pltpu.make_async_remote_copy(
            src_ref=source,
            dst_ref=target,
            send_sem=send_sem,
            recv_sem=recv_sem,
            device_id=(line, ctx),
            device_id_type=MESH,
        )

    def fetch(tile):
        slot = lax.rem(tile, 2)
        lanes = pl.ds(pl.multiple_of(tile * WIDE, WIDE), WIDE)
        return (
            pltpu.make_async_copy(proj.at[:, :, lanes], ins.at[slot, pl.ds(0, 3)], in_sem.at[slot, 0]),
            pltpu.make_async_copy(cot.at[:, lanes], ins.at[slot, 3], in_sem.at[slot, 1]),
            pltpu.make_async_copy(filt.at[:, :, lanes], fins.at[slot], in_sem.at[slot, 2]),
        )

    for tile in range(2):
        for copy in fetch(tile):
            copy.start()

    barrier = pltpu.get_barrier_semaphore()

    def greet(offset, _):
        other = lax.rem(chip + offset, CHIPS) * 2 + core
        pl.semaphore_signal(barrier, inc=1, device_id=(dp, other), device_id_type=MESH)
        return 0

    lax.fori_loop(1, CHIPS, greet, 0)
    for other in (chip * 2 + 1 - core, up, down):
        pl.semaphore_signal(barrier, inc=1, device_id=(dp, other), device_id_type=MESH)
    for offset in range(1, LINES):
        line = lax.rem(dp + offset, LINES)
        pl.semaphore_signal(barrier, inc=1, device_id=(line, me), device_id_type=MESH)

    for quarter in range(4):
        lanes = slice(quarter * 128, (quarter + 1) * 128)
        rate = rates[:, lanes]
        rows = (jnp.exp(-rate), weights[:, lanes], jnp.exp(-rate * ROWS), jnp.exp(-rate * (2 * ROWS)))
        for k in range(4):
            for again in (0, 4):
                tables[k, pl.ds(quarter + again, POLES, stride=8), :] = rows[k]

    def table(k):
        return tables[k].reshape(POLES, 8, 128)

    power = table(0)
    for k in range(8):
        powers[k] = power
        power = power * table(0)

    def short_filter(tile, t, count):
        parts = []
        for j in range(3):
            window = tiles(x.at[tile, j], t + 2, count + 6)
            weight = tiles(taps.at[tile, j], 0, TAPS)
            part = weight[0][None] * window[6 : 6 + count]
            for i in range(1, TAPS):
                part = part + weight[i][None] * window[6 - i : 6 - i + count]
            put_tiles(mix.at[tile, j], t, part)
            parts.append(part)
        return total(tiles(c.at[tile], t, count) * parts[0] * (parts[1] * parts[2]))

    def load_tile(tile):
        slot = lax.rem(tile, 2)
        for copy in fetch(tile):
            copy.wait()
        for j in range(3):
            spread(fins[slot, j], taps.at[tile, j], 0)

        def take(block):
            begin = pl.multiple_of(block * 16, 16)
            for j in range(3):
                spread(ins[slot, j, pl.ds(begin, 16), :].astype(F32), x.at[tile, j], HALO + begin)
            spread(ins[slot, 3, pl.ds(begin, 16), :].astype(F32), c.at[tile], begin)

        def inner(block, acc):
            acc = acc + short_filter(tile, block * 16 - 24, 16)
            take(block)
            return acc

        take(0)
        take(1)
        acc = lax.fori_loop(2, ROWS // 16, inner, jnp.zeros((8, 128), F32))

        @pl.when(tile < TILES - 2)
        def _():
            for copy in fetch(tile + 2):
                copy.start()

        acc = acc + short_filter(tile, ROWS - 24, 16)
        acc = acc + short_filter(tile, ROWS - 8, 8)
        gr[tile, pl.ds(21 * 8, 8), :] = acc
        gr[tile, pl.ds(22 * 8, (GRADS - 22) * 8), :] = jnp.zeros(((GRADS - 22) * 8, 128), F32)

    def load_loop(tile, _):
        load_tile(tile)
        return 0

    lax.fori_loop(0, EARLY, load_loop, 0)
    pl.semaphore_wait(barrier, CHIPS - 1 + 3 + LINES - 1)
    last, first = pl.ds(ROWS - HALO, HALO), pl.ds(0, HALO)
    halo = (
        remote(proj.at[:, last, :], prev, halo_send.at[0], halo_recv.at[0], dp, up),
        remote(proj.at[:, first, :], nextp, halo_send.at[1], halo_recv.at[1], dp, down),
        remote(cot.at[first, :], nextc, halo_send.at[2], halo_recv.at[2], dp, down),
    )
    for copy in halo:
        copy.start()
    lax.fori_loop(EARLY, TILES, load_loop, 0)
    for copy in halo:
        copy.wait()

    def plane_send(source, target, send_sem, recv_sem):
        def start(offset, _):
            other = lax.rem(chip + offset, CHIPS)
            remote(source(other), target.at[chip], send_sem, recv_sem, dp, other * 2 + core).start()
            return 0

        for offset in FAR:
            start(offset, 0)
        target[chip] = source(chip)[...]

    def plane_wait(target, send_sem, recv_sem):
        most = target.at[pl.ds(0, CHIPS - 1)]
        copy = remote(most, most, send_sem, recv_sem, dp, me)
        copy.wait_recv()
        copy.wait_send()

    pair = chip * 2 + 1 - core

    def mine(group):
        return pl.ds(pl.multiple_of((group * 2 + core) * 8, 8), 8)

    def theirs(group):
        return pl.ds(pl.multiple_of((group * 2 + 1 - core) * 8, 8), 8)

    def st_pair_copy(g):
        return remote(st.at[:, :, theirs(g), :], st_pair.at[g], st_ps.at[g], st_pr.at[g], dp, pair)

    def st_back_copy(g):
        return remote(st_give.at[g], st_land.at[g], st_ls.at[g], st_lr.at[g], dp, pair)

    def low_high(g):
        own, other = st[:, :, mine(g), :], st_pair[g]
        return jnp.where(low, own, other), jnp.where(low, other, own)

    def st_1(g):
        st_pair_copy(g).start()

    def st_2(g):
        st_pair_copy(g).wait()
        lo, hi = low_high(g)
        d = table(2)
        st_ends[g, :, 0] = d * lo[0] + hi[0]
        st_ends[g, :, 1] = lo[1] + d * hi[1]
        plane_send(lambda q: st_ends.at[g, q], st_came.at[g], st_s1.at[g], st_r1.at[g])

    def st_3(g):
        plane_wait(st_came.at[g], st_s1.at[g], st_r1.at[g])
        d2 = tables[3, pl.ds(pl.multiple_of(chip * 8, 8), 8), :]
        s = jnp.zeros((8, 128), F32)
        for q in range(CHIPS):
            st_back[g, q, 0] = s
            s = d2 * s + st_came[g, q, 0]
        s = jnp.zeros((8, 128), F32)
        for q in reversed(range(CHIPS)):
            st_back[g, q, 1] = s
            s = d2 * s + st_came[g, q, 1]
        plane_send(lambda q: st_back.at[g, q], st_enter.at[g], st_s2.at[g], st_r2.at[g])

    def st_4(g):
        plane_wait(st_enter.at[g], st_s2.at[g], st_r2.at[g])
        lo, hi = low_high(g)
        d = table(2)
        fwd, bwd = st_enter[g, :, 0], st_enter[g, :, 1]
        fwd_hi, bwd_lo = d * fwd + lo[0], d * bwd + hi[1]
        st[0, :, mine(g), :] = jnp.where(low, fwd, fwd_hi)
        st[1, :, mine(g), :] = jnp.where(low, bwd_lo, bwd)
        st_give[g, 0] = jnp.where(low, fwd_hi, fwd)
        st_give[g, 1] = jnp.where(low, bwd, bwd_lo)
        st_back_copy(g).start()

    def st_5(g):
        st_back_copy(g).wait()
        st[:, :, theirs(g), :] = st_land[g]

    def st_hooks(slot):
        step = lax.div(slot, 2)
        even = lax.rem(slot, 2) == 0

        @pl.when(jnp.logical_and(even, jnp.logical_and(step >= 1, step < GROUPS + 1)))
        def _():
            st_2(step - 1)

        @pl.when(jnp.logical_and(even, jnp.logical_and(step >= 2, step < GROUPS + 2)))
        def _():
            st_3(step - 2)

        @pl.when(jnp.logical_and(even, jnp.logical_and(step >= 3, step < GROUPS + 3)))
        def _():
            st_4(step - 3)

    def local_scan(tile):
        q, k, v = mix.at[tile, 0], mix.at[tile, 1], mix.at[tile, 2]
        rows = pl.ds(pl.multiple_of(tile * 8, 8), 8)
        gain = skip[rows, :][None]

        def step(block, carry):
            s, b = carry
            begin, end = block * 8, EXT - 8 - block * 8
            a, r = table(0), table(1)
            g = tiles(k, begin, 8) * tiles(v, begin, 8)
            gf = tiles(c.at[tile], end, 8) * tiles(q, end, 8)
            fwd, bwd = [], []
            for u in range(8):
                s = a * s + g[u][None]
                b = a * b + gf[7 - u][None]
                fwd.append(total(r * s))
                bwd.append(total(r * b))
            put_tiles(yf.at[tile], begin, jnp.stack(fwd) + gain * g)
            put_tiles(yb.at[tile], end, jnp.stack(bwd[::-1]) + gain * gf)
            return s, b

        zero = jnp.zeros((POLES, 8, 128), F32)
        s, b = lax.fori_loop(0, ROWS // 8, step, (zero, zero))
        st[0, :, rows, :] = s
        st[1, :, rows, :] = b
        lax.fori_loop(ROWS // 8, EXT // 8, step, (s, b))

    def scan_loop(tile, _):
        lanes = pl.ds(pl.multiple_of(tile * WIDE, WIDE), WIDE)
        for j in range(3):
            spread(prev[j, :, lanes].astype(F32) * has_prev, x.at[tile, j], 0)
            spread(nextp[j, :, lanes].astype(F32) * has_next, x.at[tile, j], HALO + ROWS)
        spread(nextc[:, lanes].astype(F32) * has_next, c.at[tile], ROWS)

        gr[tile, pl.ds(21 * 8, 8), :] += short_filter(tile, 0, 8)
        short_filter(tile, ROWS, 8)
        local_scan(tile)

        @pl.when(lax.rem(tile, 2) == 1)
        def _():
            st_1(lax.div(tile, 2))

        st_hooks(tile)
        return 0

    lax.fori_loop(0, TILES, scan_loop, 0)

    def gr_half(h, which):
        begin, many, rows = SUMS[h]
        half = many // 2
        return gr.at[pl.ds(begin + which * half, half), pl.ds(0, rows * 8), :]

    def gr_pair_copy(h):
        return remote(gr_half(h, 1 - core), gr_pair[h], gr_ps.at[h, 0], gr_pr.at[h, 0], dp, pair)

    def gr_back_copy(h):
        return remote(gr_around[h], gr_land[h], gr_ps.at[h, 1], gr_pr.at[h, 1], dp, pair)

    def gr_1(h):
        gr_pair_copy(h).start()

    def gr_2(h):
        gr_pair_copy(h).wait()
        both = gr_half(h, core)[...] + gr_pair[h][...]
        gr_cut[h][...] = both.reshape(CHIPS, PIECES[h], 128)
        plane_send(lambda q: gr_cut[h].at[q], gr_came[h], gr_s1.at[h], gr_r1.at[h])

    def line_copy(h, other, slot):
        return remote(gr_part[h], gr_lines[h].at[slot], gr_ls.at[h, other], gr_lr.at[h, slot], other, me)

    def gr_3(h):
        plane_wait(gr_came[h], gr_s1.at[h], gr_r1.at[h])
        part = gr_came[h][0]
        for q in range(1, CHIPS):
            part = part + gr_came[h][q]
        gr_part[h][...] = part
        gr_lines[h][dp] = part
        for offset in range(1, LINES):
            line_copy(h, lax.rem(dp + offset, LINES), dp).start()

    def gr_4(h):
        for offset in range(1, LINES):
            other = lax.rem(dp + offset, LINES)
            line_copy(h, other, other).wait_recv()
            line_copy(h, other, dp).wait_send()
        part = gr_lines[h][0]
        for q in range(1, LINES):
            part = part + gr_lines[h][q]
        gr_whole[h][...] = part
        plane_send(lambda q: gr_whole[h], gr_around[h], gr_s2.at[h], gr_r2.at[h])

    def gr_5(h):
        plane_wait(gr_around[h], gr_s2.at[h], gr_r2.at[h])
        gr_back_copy(h).start()

    def gr_6(h):
        gr_back_copy(h).wait()
        _, many, rows = SUMS[h]
        gr_half(h, core)[...] = gr_around[h][...].reshape(many // 2, rows * 8, 128)
        gr_half(h, 1 - core)[...] = gr_land[h][...].reshape(many // 2, rows * 8, 128)

    def correct(tile):
        q, k_ref, v = mix.at[tile, 0], mix.at[tile, 1], mix.at[tile, 2]
        rows = pl.ds(pl.multiple_of(tile * 8, 8), 8)

        def step(block, carry):
            e, b = carry
            begin, end = block * 8, EXT - 8 - block * 8
            ahead, behind = [], []
            for k in range(8):
                fwd, bwd = 0, 0
                for n in range(0, POLES, 4):
                    weight = powers[k, n : n + 4]
                    fwd = fwd + weight * e[n : n + 4]
                    bwd = bwd + weight * b[n : n + 4]
                ahead.append(total(fwd))
                behind.append(total(bwd))
            filtered = tiles(yf.at[tile], begin, 8) + jnp.stack(ahead)
            grad_gated = tiles(yb.at[tile], end, 8) + jnp.stack(behind[::-1])
            query, upstream = tiles(q, begin, 8), tiles(c.at[tile], begin, 8)
            key, value = tiles(k_ref, end, 8), tiles(v, end, 8)
            put_tiles(yf.at[tile], begin, query * filtered)
            put_tiles(c.at[tile], begin, upstream * filtered)
            put_tiles(k_ref, end, grad_gated * value)
            put_tiles(v, end, grad_gated * key)
            return powers[7] * e, powers[7] * b

        r = table(1)
        lax.fori_loop(0, EXT // 8, step, (r * st[0, :, rows, :], r * st[1, :, rows, :]))

    def mixed_grad(tile, j):
        return c.at[tile] if j == 0 else mix.at[tile, j]

    def tap_grads(tile):
        for j in range(3):

            def body(block, acc):
                t = block * 16
                grad = tiles(mixed_grad(tile, j), t, 16)
                window = tiles(x.at[tile, j], t + 2, 22)
                return tuple(acc[i] + total(grad * window[6 - i : 22 - i]) for i in range(TAPS))

            acc = lax.fori_loop(0, ROWS // 16, body, (jnp.zeros((8, 128), F32),) * TAPS)
            for i in range(TAPS):
                gr[tile, pl.ds((j * TAPS + i) * 8, 8), :] = acc[i]

    stages = (gr_1, gr_2, gr_3, gr_4, gr_5, gr_6)
    plan = {
        3: ((1, 0),),
        5: ((2, 0), (1, 1)),
        6: ((2, 1),),
        7: ((1, 2), (3, 0)),
        8: ((2, 2), (3, 1)),
        9: ((4, 0),),
        11: ((4, 1),),
        12: ((3, 2),),
        13: ((5, 0),),
        15: ((4, 2), (6, 0), (5, 1)),
    }

    def gr_hooks(tile, offset):
        for slot, todo in plan.items():
            if offset <= slot < offset + TILES:

                @pl.when(tile == slot - offset)
                def _(todo=todo):
                    for stage, h in todo:
                        stages[stage - 1](h)

    def post_loop(tile, _):
        @pl.when(lax.rem(tile, 2) == 0)
        def _():
            st_5(lax.div(tile, 2))

        correct(tile)
        tap_grads(tile)
        st_hooks(tile + TILES)
        gr_hooks(tile, 0)
        return 0

    lax.fori_loop(0, TILES, post_loop, 0)

    def out_loop(tile, _):
        def filter_rows(j, block):
            t = block * 16
            ahead = tiles(mixed_grad(tile, j), t, 22)
            weight = tiles(taps.at[tile, j], 0, TAPS)
            part = weight[0][None] * ahead[0:16]
            for i in range(1, TAPS):
                part = part + weight[i][None] * ahead[i : i + 16]
            put_tiles(x.at[tile, j], t, part)

        def give(source, j, block):
            begin = pl.multiple_of(block * 16, 16)
            for lane in range(8):
                value = source[pl.ds(begin * 8 + lane, 16, stride=8), :]
                lanes = pl.ds(pl.multiple_of(tile * WIDE + lane * 128, 128), 128)
                outs[j, pl.ds(begin, 16), lanes] = value.astype(BF16)

        def body(block, _):
            for j in range(3):
                give(x.at[tile, j], j, block - 1)
            give(yf.at[tile], 3, block)
            for j in range(3):
                filter_rows(j, block)
            return 0

        for j in range(3):
            filter_rows(j, 0)
        give(yf.at[tile], 3, 0)
        lax.fori_loop(1, ROWS // 16, body, 0)
        for j in range(3):
            give(x.at[tile, j], j, ROWS // 16 - 1)

        gr_hooks(tile, TILES)
        return 0

    lax.fori_loop(0, TILES, out_loop, 0)
    gr_6(1)
    gr_5(2)
    gr_6(2)


def leave_kernel(outs, gr, output, grad_proj, grad_short, grad_skip, sem):
    copies = [
        pltpu.make_async_copy(outs.at[j], grad_proj.at[j], sem.at[j]) for j in range(3)
    ] + [pltpu.make_async_copy(outs.at[3], output, sem.at[3])]
    for copy in copies:
        copy.start()
    for tile in range(TILES):
        grad_skip[tile * 8 : tile * 8 + 8, :] = gr[tile, 21 * 8 : 22 * 8, :]
        for j in range(3):
            for lane in range(8):
                value = gr[tile, pl.ds(j * TAPS * 8 + lane, TAPS, stride=8), :]
                begin = tile * WIDE + lane * 128
                grad_short[j, :, begin : begin + 128] = value
    for copy in copies:
        copy.wait()


def leave(outs, gr):
    channels = outs.shape[2]
    anywhere = pl.BlockSpec(memory_space=pl.ANY)
    vmem = pl.BlockSpec(memory_space=pltpu.VMEM)
    return pl.pallas_call(
        leave_kernel,
        name="leave",
        out_shape=(
            jax.ShapeDtypeStruct((ROWS, channels), BF16),
            jax.ShapeDtypeStruct((3, ROWS, channels), BF16),
            jax.ShapeDtypeStruct((3, TAPS, channels), F32),
            jax.ShapeDtypeStruct((TILES * 8, 128), F32),
        ),
        in_specs=[vmem, vmem],
        out_specs=(anywhere, anywhere, vmem, vmem),
        scratch_shapes=[pltpu.SemaphoreType.DMA((4,))],
        compiler_params=pltpu.CompilerParams(vmem_limit_bytes=4 << 20),
    )(
        pltpu.with_memory_space_constraint(outs, pltpu.VMEM),
        pltpu.with_memory_space_constraint(gr, pltpu.VMEM),
    )


def whole(proj, cot, filt, skip, rates, weights):
    channels = proj.shape[2]
    anywhere = pl.BlockSpec(memory_space=pl.ANY)
    vmem = pl.BlockSpec(memory_space=pltpu.VMEM)

    def buffer(*shape, kind=F32):
        return pltpu.VMEM(shape, kind)

    def dma(*shape):
        return pltpu.SemaphoreType.DMA(shape)

    slots = tuple(buffer(CHIPS, piece, 128) for piece in PIECES)
    pieces = tuple(buffer(piece, 128) for piece in PIECES)
    return pl.pallas_call(
        kernel,
        name="hyena",
        out_shape=(
            buffer(4, ROWS, channels, kind=BF16),
            buffer(TILES, GRADS * 8, 128),
        ),
        in_specs=[anywhere, anywhere, anywhere, vmem, vmem, vmem],
        out_specs=(vmem, vmem),
        scratch_shapes=[
            buffer(TILES, 3, (EXT + HALO) * 8, 128),
            buffer(TILES, 3, EXT * 8, 128),
            buffer(TILES, EXT * 8, 128),
            buffer(TILES, EXT * 8, 128),
            buffer(TILES, EXT * 8, 128),
            buffer(2, 4, ROWS, WIDE, kind=BF16),
            buffer(2, 3, TAPS, WIDE),
            buffer(3, HALO, channels, kind=BF16),
            buffer(3, HALO, channels, kind=BF16),
            buffer(HALO, channels, kind=BF16),
            buffer(TILES, 3, TAPS * 8, 128),
            buffer(4, POLES * 8, 128),
            buffer(8, POLES, 8, 128),
            buffer(2, POLES, TILES * 8, 128),
            buffer(GROUPS, 2, POLES, 8, 128),
            buffer(GROUPS, CHIPS, 2, 8, 128),
            buffer(GROUPS, CHIPS, 2, 8, 128),
            buffer(GROUPS, CHIPS, 2, 8, 128),
            buffer(GROUPS, CHIPS, 2, 8, 128),
            buffer(GROUPS, 2, POLES, 8, 128),
            buffer(GROUPS, 2, POLES, 8, 128),
            tuple(buffer(many // 2, rows * 8, 128) for _, many, rows in SUMS),
            slots,
            slots,
            pieces,
            pieces,
            tuple(buffer(LINES, piece, 128) for piece in PIECES),
            slots,
            slots,
            dma(2, 3),
            dma(3),
            dma(3),
        ]
        + [dma(GROUPS)] * 8
        + [dma(len(SUMS), 2)] * 2
        + [dma(len(SUMS))] * 4
        + [dma(len(SUMS), LINES)] * 2,
        compiler_params=pltpu.CompilerParams(
            collective_id=0, has_side_effects=True, vmem_limit_bytes=52 << 20
        ),
    )(proj, cot, filt, skip, rates, weights)


def local(projected, short_filter, residues, decay_rates, skip_gain, cotangent):
    proj = jnp.transpose(projected[0], (1, 0, 2))
    skip = skip_gain.reshape(TILES * 8, 128)
    outs, grads = whole(proj, cotangent[0], short_filter, skip, decay_rates.T, residues.T)
    output, grad_proj, grad_short, grad_skip = leave(outs, grads)
    return (
        output[None],
        jnp.transpose(grad_proj, (1, 0, 2))[None],
        grad_short,
        grad_skip.reshape(skip_gain.shape),
    )


def solution(mesh):
    placed = (P("dp", "ctx", None, None), P(), P(), P(), P(), P("dp", "ctx", None))
    return jax.shard_map(
        local,
        mesh=mesh,
        in_specs=placed,
        out_specs=(P("dp", "ctx", None), P("dp", "ctx", None, None), P(), P()),
        check_vma=False,
    )
```
